512 devices in a mesh: row: 8 (over z_lo, core), col: 8 (over x, z_hi), tm: 8 (over y).
Axes of the slice: x: 4, y: 8, z: 8 (z_hi: 2, z_lo: 4; z = z_hi * 4 + z_lo), core: 2. Of those that a mesh axis runs over, the one named last changes fastest.
Arguments:
- green_occ: bfloat16 [16, 256, 30720], P('tm', 'row', 'col'), may hold values from -6 to 6
- green_virt: bfloat16 [16, 256, 30720], P('tm', 'row', 'col'), may hold values from -6 to 6
- adjoint_w: bfloat16 [16, 256, 30720], P(None, 'row', ('col', 'tm')), may hold values from -6 to 6
- grad_basis: float32 [3, 256], P(None, 'row'), may hold values from -6 to 6
- owner_map: int32 [30720], replicated, may hold values from 0 to 999
- block_offset: int32 [8], P('row'), may hold values from 0 to 30688
Outputs:
- chi_freq: bfloat16 [16, 256, 30720], P(None, 'row', ('col', 'tm'))
- forces: float32 [3, 1000], replicated
The draws below stay inside these ranges and needn't reach their ends.
All inputs are finite; a program needn't handle non-finite values.
Results may differ from the reference program's by a relative error of at most 0.0085.
Values may be sent and summed in bfloat16 or wider, within the bound.
No kernel may reach another device: no remote copies, remote signals or barrier semaphores. Data moves between devices by JAX's collectives and lax.ppermute only.
A program may use at most 64 MiB of HBM per device.

```python
import math
import jax
import jax.numpy as jnp
from jax import lax

NG = 30720
NTAU = 16
NATOM = 1000
ROW_DEV = 32
ROWS = 256
N_ROW = 8


def set_ends(values, stream_key, smallest, top_value):
    shape = values.shape
    spot = [jax.random.randint(jax.random.fold_in(stream_key, axis), (), 0, shape[axis]) for axis in range(len(shape))]
    values = values.at[tuple(spot)].set(smallest)
    longest = shape.index(max(shape))
    spot[longest] = (spot[longest] + 1) % shape[longest]
    return values.at[tuple(spot)].set(top_value)


def shard_levels(rng, shape, cuts, smallest, high):
    loudness = 1.0
    for position, parts in cuts:
        steps = jax.random.uniform(jax.random.fold_in(jax.random.fold_in(rng, 6), position), (parts,), jnp.float32, smallest / len(cuts), high / len(cuts))
        loudness = loudness * jnp.repeat(jnp.exp(steps), shape[position] // parts).reshape((-1,) + (1,) * (len(shape) - 1 - position))
    return loudness


def bell_draw(own_key, shape, width, most, shards=(), kind=jnp.bfloat16):
    factor_of = shard_levels(own_key, shape, shards, -0.22, 0.18) if shards else 1.0
    drawn = jax.random.normal(own_key, shape, jnp.float32) * width * factor_of
    return jnp.minimum(jnp.maximum(drawn, -most), most).astype(kind)


def setup_inputs(seed: int = 0) -> dict:
    key_list = jax.random.split(jax.random.key(seed), 7)
    return {
        "green_occ": bell_draw(key_list[0], (NTAU, ROWS, NG), 1.0, 6.0, ((0, 8), (1, 8), (2, 8))),
        "green_virt": bell_draw(key_list[1], (NTAU, ROWS, NG), 1.0, 6.0, ((0, 8), (1, 8), (2, 8))),
        "adjoint_w": bell_draw(key_list[2], (NTAU, ROWS, NG), 1.0, 6.0, ((1, 8), (2, 64))),
        "grad_basis": bell_draw(key_list[3], (3, ROWS), 1.0, 6.0, ((1, 8),), jnp.float32),
        "owner_map": set_ends(jax.random.randint(key_list[4], (NG,), 0, NATOM), jax.random.fold_in(key_list[4], 1), 0, NATOM - 1).astype(jnp.int32),
        "block_offset": set_ends(jax.random.randint(key_list[5], (N_ROW,), 0, NG - ROW_DEV + 1), jax.random.fold_in(key_list[5], 1), 0, NG - ROW_DEV).astype(jnp.int32),
    }


def cos_table(count):
    steps = jnp.arange(count).astype(jnp.float32)
    tau = 0.1 * jnp.power(jnp.float32(1.35), steps)
    omega = 0.15 * jnp.power(jnp.float32(1.35), steps)
    return jnp.cos(omega[:, None] * tau[None, :]) / 4.0

def reference(green_occ, green_virt, adjoint_w, grad_basis, owner_map, block_offset):
    table = cos_table(NTAU)
    scale = 1.0 / math.sqrt(NTAU * NG)

    def one_block(index):
        start = (index * ROW_DEV).astype(jnp.int32)
        occ = lax.dynamic_slice_in_dim(green_occ, start, ROW_DEV, 1)
        virt = lax.dynamic_slice_in_dim(green_virt, start, ROW_DEV, 1)
        adj = lax.dynamic_slice_in_dim(adjoint_w, start, ROW_DEV, 1)
        prod = (occ.astype(jnp.float32) * virt.astype(jnp.float32)).astype(jnp.bfloat16)
        chi = jnp.einsum('kt,trc->krc', table, prod.astype(jnp.float32), precision=lax.Precision.HIGHEST).astype(jnp.bfloat16)
        energy = lax.optimization_barrier(jnp.sum(adj.astype(jnp.float32) * chi.astype(jnp.float32), axis=(0, 2))) * scale
        return (chi, energy)
    chis, energies = lax.map(one_block, jnp.arange(N_ROW).astype(jnp.int32))
    chi_freq = jnp.transpose(chis, (1, 0, 2, 3)).reshape(NTAU, ROWS, NG)
    points = (block_offset[:, None] + jnp.arange(ROW_DEV).astype(jnp.int32)[None, :]).reshape(ROWS)
    owners = owner_map[points]
    onehot = (owners[:, None] == jnp.arange(NATOM).astype(jnp.int32)[None, :]).astype(jnp.float32)
    weighted = grad_basis * energies.reshape(ROWS)[None, :]
    forces = jnp.dot(weighted, onehot, precision=lax.Precision.HIGHEST, preferred_element_type=jnp.float32)
    return (chi_freq, forces)
```

```python
import functools
import math

import jax
import jax.numpy as jnp
import ml_dtypes
import numpy as np
from jax import lax
from jax.experimental import pallas as pl
from jax.experimental.pallas import tpu as pltpu
from jax.sharding import PartitionSpec as P

NG = 30720
NTAU = 16
NATOM = 1000
GROUP = 16
LANES = 128


def transform_matrix():
    steps = np.arange(NTAU, dtype=np.float64)
    tau = 0.1 * 1.35**steps
    omega = 0.15 * 1.35**steps
    table = np.cos(omega[:, None] * tau[None, :]) / 4.0
    high = table.astype(ml_dtypes.bfloat16)
    low = (table - high.astype(np.float64)).astype(ml_dtypes.bfloat16)
    eye = np.eye(GROUP)
    return [np.kron(part.astype(np.float64), eye).astype(ml_dtypes.bfloat16) for part in (high, low)]


def product_kernel(n_dest, occ_ref, virt_ref, out_ref):
    width = out_ref.shape[-1]
    product = occ_ref[0].astype(jnp.float32) * virt_ref[0].astype(jnp.float32)
    for j in range(n_dest):
        out_ref[j, 0] = product[:, j * width : (j + 1) * width].astype(jnp.bfloat16)


def transform_kernel(n_copies, high_ref, low_ref, prod_ref, adj_ref, chi_ref, energy_ref):
    n_freq, rows, width = chi_ref.shape
    total = jnp.zeros((1, LANES), jnp.float32)
    for start in range(0, rows, GROUP):
        block = pl.ds(start, GROUP)
        times = prod_ref[:, block, :].reshape(NTAU * GROUP, width)
        chi = jnp.dot(high_ref[...], times, preferred_element_type=jnp.float32)
        chi += jnp.dot(low_ref[...], times, preferred_element_type=jnp.float32)
        chi = chi.reshape(n_freq, GROUP, width).astype(jnp.bfloat16)
        chi_ref[:, block, :] = chi
        terms = adj_ref[:, block, :].astype(jnp.float32) * chi.astype(jnp.float32)
        energy = jnp.sum(jnp.sum(terms, axis=0), axis=1, keepdims=True)
        row = lax.broadcasted_iota(jnp.int32, (GROUP, LANES), 0) + start
        lane = lax.broadcasted_iota(jnp.int32, (GROUP, LANES), 1)
        spread = jnp.where(lane % rows == row, energy, 0.0)
        total += jnp.sum(spread, axis=0, keepdims=True)
    energy_ref[...] = jnp.broadcast_to(total, (n_copies, LANES))


def forces_kernel(rows, message_ref, forces_ref):
    n_block = message_ref.shape[0]
    messages = message_ref[...]
    weighted = jnp.sum(messages, axis=1)
    first = messages[:, 0, :]

    def along_lanes(values, part):
        return jnp.concatenate(
            [values[i : i + 1, part * rows : (part + 1) * rows] for i in range(n_block)], axis=1
        )

    weights = jnp.concatenate([along_lanes(weighted, part) for part in range(3)], axis=0)
    owners = along_lanes(first, 3).astype(jnp.int32)
    atoms = lax.broadcasted_iota(jnp.int32, (NATOM, owners.shape[1]), 0)
    onehot = jnp.where(atoms == owners, 1.0, 0.0).astype(jnp.bfloat16)
    rest = weights
    forces = jnp.zeros((3, NATOM), jnp.float32)
    for _ in range(3):
        part = rest.astype(jnp.bfloat16)
        rest = rest - part.astype(jnp.float32)
        forces += lax.dot_general(
            part, onehot, (((1,), (1,)), ((), ())), preferred_element_type=jnp.float32
        )
    forces_ref[...] = forces


def on_device(sizes, green_occ, green_virt, adjoint_w, grad_basis, owner_map, block_offset):
    n_row, n_col, n_tm = sizes
    n_time, rows, columns = green_occ.shape
    width = columns // n_tm
    scale = 1.0 / math.sqrt(NTAU * NG)
    high, low = transform_matrix()

    product = pl.pallas_call(
        functools.partial(product_kernel, n_tm),
        grid=(n_time,),
        in_specs=[pl.BlockSpec((1, rows, columns), lambda t: (t, 0, 0))] * 2,
        out_specs=pl.BlockSpec((n_tm, 1, rows, width), lambda t: (0, t, 0, 0)),
        out_shape=jax.ShapeDtypeStruct((n_tm, n_time, rows, width), jnp.bfloat16),
        name="product",
    )(green_occ, green_virt)
    times = lax.all_to_all(product, "tm", split_axis=0, concat_axis=0, tiled=True)
    times = times.reshape(NTAU, rows, width)

    owners = lax.dynamic_slice_in_dim(owner_map, block_offset[0], rows, 0)
    weight = jnp.concatenate([grad_basis.reshape(3 * rows) * scale, jnp.zeros((rows,), jnp.float32)])
    label = jnp.concatenate([jnp.zeros((3 * rows,), jnp.float32), owners.astype(jnp.float32)])

    chi_freq, energy = pl.pallas_call(
        functools.partial(transform_kernel, n_tm),
        out_shape=(
            jax.ShapeDtypeStruct((NTAU, rows, width), jnp.bfloat16),
            jax.ShapeDtypeStruct((n_tm, LANES), jnp.float32),
        ),
        compiler_params=pltpu.CompilerParams(vmem_limit_bytes=32 << 20),
        name="transform",
    )(jnp.asarray(high), jnp.asarray(low), times, adjoint_w)

    energy = lax.all_to_all(energy, "tm", split_axis=0, concat_axis=0, tiled=True)
    message = jnp.sum(energy, axis=0) * weight + label
    message = jnp.broadcast_to(message[None, :], (n_row * n_col, LANES))
    message = lax.all_to_all(message, ("row", "col"), split_axis=0, concat_axis=0, tiled=True)
    forces = pl.pallas_call(
        functools.partial(forces_kernel, rows),
        out_shape=jax.ShapeDtypeStruct((3, NATOM), jnp.float32),
        compiler_params=pltpu.CompilerParams(vmem_limit_bytes=32 << 20),
        name="forces",
    )(message.reshape(n_row, n_col, LANES))
    return (chi_freq, forces)


def solution(mesh):
    in_specs = (
        P("tm", "row", "col"),
        P("tm", "row", "col"),
        P(None, "row", ("col", "tm")),
        P(None, "row"),
        P(),
        P("row"),
    )
    out_specs = (P(None, "row", ("col", "tm")), P())
    sizes = tuple(mesh.shape[name] for name in ("row", "col", "tm"))
    return jax.shard_map(
        functools.partial(on_device, sizes),
        mesh=mesh,
        in_specs=in_specs,
        out_specs=out_specs,
        check_vma=False,
    )
```

```python
import functools
import math

import jax
import jax.numpy as jnp
import ml_dtypes
import numpy as np
from jax import lax
from jax.experimental import pallas as pl
from jax.experimental.pallas import tpu as pltpu
from jax.sharding import Mesh, PartitionSpec as P

NG = 30720
NTAU = 16
NATOM = 1000
GROUP = 16
LANES = 128
CORES = 2


def transform_matrix():
    steps = np.arange(NTAU, dtype=np.float64)
    table = np.cos(0.1 * 0.15 * 1.35 ** (steps[:, None] + steps[None, :])) / 4.0
    high = table.astype(ml_dtypes.bfloat16)
    low = (table - high.astype(np.float64)).astype(ml_dtypes.bfloat16)
    eye = np.eye(GROUP)
    return [np.kron(part.astype(np.float64), eye).astype(ml_dtypes.bfloat16) for part in (high, low)]


def product_kernel(chunks, occ_ref, virt_ref, out_ref, occ, virt, out, in_sems, out_sems):
    n_dest, _, _, width = out_ref.shape
    loads, stores = [], []
    for i, (t, rows) in enumerate(chunks):
        pair = [
            pltpu.make_async_copy(src.at[t, rows], dst.at[t, rows], in_sems.at[i, s])
            for s, (src, dst) in enumerate(((occ_ref, occ), (virt_ref, virt)))
        ]
        for load in pair:
            load.start()
        loads.append(pair)
    for i, (t, rows) in enumerate(chunks):
        for load in loads[i]:
            load.wait()
        product = occ[t, rows].astype(jnp.float32) * virt[t, rows].astype(jnp.float32)
        for j in range(n_dest):
            out[j, t, rows] = product[:, j * width : (j + 1) * width].astype(jnp.bfloat16)
        store = pltpu.make_async_copy(out.at[:, t, rows], out_ref.at[:, t, rows], out_sems.at[i])
        store.start()
        stores.append(store)
    for store in stores:
        store.wait()


def transform_kernel(high_ref, low_ref, in_ref, out_ref):
    n_out, rows, width = out_ref.shape
    for start in range(0, rows, GROUP):
        block = pl.ds(start, GROUP)
        terms = in_ref[:, block, :].reshape(NTAU * GROUP, width)
        total = jnp.dot(high_ref[...], terms, preferred_element_type=jnp.float32)
        total += jnp.dot(low_ref[...], terms, preferred_element_type=jnp.float32)
        out_ref[:, block, :] = total.reshape(n_out, GROUP, width).astype(out_ref.dtype)


def energy_kernel(prod_ref, adjoint_ref, weight_ref, label_ref, message_ref):
    n_time, rows, _ = prod_ref.shape
    terms = prod_ref[0].astype(jnp.float32) * adjoint_ref[0]
    for t in range(1, n_time):
        terms += prod_ref[t].astype(jnp.float32) * adjoint_ref[t]
    energy = jnp.sum(terms, axis=1, keepdims=True)
    row = lax.broadcasted_iota(jnp.int32, (rows, LANES), 0)
    lane = lax.broadcasted_iota(jnp.int32, (rows, LANES), 1)
    spread = jnp.sum(jnp.where(lane % rows == row, energy, 0.0), axis=0, keepdims=True)
    message = spread * weight_ref[...] + label_ref[...]
    message_ref[...] = jnp.broadcast_to(message, message_ref.shape)


def forces_kernel(rows, n_col, message_ref, forces_ref):
    sums = []
    for block in range(message_ref.shape[0] // n_col * CORES):
        pair, core = divmod(block, CORES)
        devices = pl.ds(pair * n_col, n_col)
        sums.append(jnp.sum(message_ref[devices, core, :], axis=0, keepdims=True))
    parts = [
        jnp.concatenate([total[:, p * rows : (p + 1) * rows] for total in sums], axis=1)
        for p in range(4)
    ]
    owners = parts[3].astype(jnp.int32)
    weights = jnp.concatenate(parts[:3] + [jnp.zeros_like(parts[0])] * 5, axis=0)
    upper, lower = owners // LANES, owners % LANES
    n_upper = pl.cdiv(NATOM, LANES)
    rest = jnp.concatenate([jnp.where(upper == u, weights, 0.0) for u in range(n_upper)], axis=0)
    lanes = lax.broadcasted_iota(jnp.int32, (LANES, owners.shape[1]), 0)
    onehot = jnp.where(lanes == lower, 1.0, 0.0).astype(jnp.bfloat16)
    forces = jnp.zeros((8 * n_upper, LANES), jnp.float32)
    for _ in range(3):
        part = rest.astype(jnp.bfloat16)
        rest = rest - part.astype(jnp.float32)
        forces += lax.dot_general(
            part, onehot, (((1,), (1,)), ((), ())), preferred_element_type=jnp.float32
        )
    for u in range(n_upper):
        count = min(LANES, NATOM - u * LANES)
        forces_ref[:, u * LANES : u * LANES + count] = forces[u * 8 : u * 8 + 3, :count]


def on_device(sizes, green_occ, green_virt, adjoint_w, grad_basis, owner_map, block_offset):
    n_pair, n_col, n_tm = sizes
    n_time, rows, columns = green_occ.shape
    width = columns // n_tm
    scale = 1.0 / math.sqrt(NTAU * NG)
    high, low = (jnp.asarray(part) for part in transform_matrix())
    shape = (NTAU, rows, width)

    half = rows // 2
    chunks = [(t, pl.ds(start, half)) for t in range(n_time) for start in (0, half)]
    product = pl.pallas_call(
        functools.partial(product_kernel, chunks),
        in_specs=[pl.BlockSpec(memory_space=pl.ANY)] * 2,
        out_specs=pl.BlockSpec(memory_space=pl.ANY),
        out_shape=jax.ShapeDtypeStruct((n_tm, n_time, rows, width), jnp.bfloat16),
        scratch_shapes=[
            pltpu.VMEM(green_occ.shape, jnp.bfloat16),
            pltpu.VMEM(green_virt.shape, jnp.bfloat16),
            pltpu.VMEM((n_tm, n_time, rows, width), jnp.bfloat16),
            pltpu.SemaphoreType.DMA((len(chunks), 2)),
            pltpu.SemaphoreType.DMA((len(chunks),)),
        ],
        name="product",
    )(green_occ, green_virt)
    times = lax.all_to_all(product, "tm", split_axis=0, concat_axis=0, tiled=True).reshape(shape)

    def transform(name, values, dtype):
        return pl.pallas_call(
            transform_kernel,
            out_shape=jax.ShapeDtypeStruct(shape, dtype),
            cost_estimate=pl.CostEstimate(
                flops=4 * NTAU * GROUP * rows * NTAU * width,
                bytes_accessed=(2 + jnp.dtype(dtype).itemsize) * NTAU * rows * width,
                transcendentals=0,
            ),
            compiler_params=pltpu.CompilerParams(vmem_limit_bytes=16 << 20),
            name=name,
        )(high, low, values)

    owners = lax.dynamic_slice_in_dim(owner_map, block_offset[0], rows, 0)
    weight = jnp.concatenate([grad_basis.reshape(3 * rows) * scale, jnp.zeros((rows,), jnp.float32)])
    label = jnp.concatenate(
        [jnp.zeros((3 * rows,), jnp.float32), owners.astype(jnp.float32) * (1.0 / (n_col * n_tm))]
    )
    adjoint_time = transform("adjoint_time", adjoint_w, jnp.float32)
    message = pl.pallas_call(
        energy_kernel,
        out_shape=jax.ShapeDtypeStruct((CORES * n_tm, LANES), jnp.float32),
        compiler_params=pltpu.CompilerParams(vmem_limit_bytes=16 << 20),
        name="energy",
    )(times, adjoint_time, weight[None, :], label[None, :])

    message = lax.all_to_all(message, ("core", "tm"), split_axis=0, concat_axis=0, tiled=True)
    chi_freq = transform("chi_freq", times, jnp.bfloat16)
    message = jnp.sum(message.reshape(CORES, n_tm, LANES), axis=1)
    message = jnp.broadcast_to(message[None], (n_pair * n_col, CORES, LANES))
    message = lax.all_to_all(message, ("pair", "col"), split_axis=0, concat_axis=0, tiled=True)
    forces = pl.pallas_call(
        functools.partial(forces_kernel, rows, n_col),
        out_shape=jax.ShapeDtypeStruct((3, NATOM), jnp.float32),
        compiler_params=pltpu.CompilerParams(vmem_limit_bytes=8 << 20),
        name="forces",
    )(message)
    return (chi_freq, forces)


def solution(mesh):
    n_row, n_col, n_tm = (mesh.shape[name] for name in ("row", "col", "tm"))
    n_pair = n_row // CORES
    fine = Mesh(mesh.devices.reshape(n_pair, CORES, n_col, n_tm), ("pair", "core", "col", "tm"))
    row = ("pair", "core")
    in_specs = (
        P("tm", row, "col"),
        P("tm", row, "col"),
        P(None, row, ("col", "tm")),
        P(None, row),
        P(),
        P(row),
    )
    out_specs = (P(None, row, ("col", "tm")), P())
    return jax.shard_map(
        functools.partial(on_device, (n_pair, n_col, n_tm)),
        mesh=fine,
        in_specs=in_specs,
        out_specs=out_specs,
        check_vma=False,
    )
```

```python
import functools
import math

import jax
import jax.numpy as jnp
import ml_dtypes
import numpy as np
from jax import lax
from jax.experimental import pallas as pl
from jax.experimental.pallas import tpu as pltpu
from jax.sharding import Mesh, PartitionSpec as P

NG = 30720
NTAU = 16
NATOM = 1000
GROUP = 16
LANES = 128
SHIFT = 32
QUARTERS = LANES // SHIFT
FULL = 3
CORES = 2


def transform_matrix():
    steps = np.arange(NTAU, dtype=np.float64)
    table = np.cos(0.1 * 0.15 * 1.35 ** (steps[:, None] + steps[None, :])) / 4.0
    high = table.astype(ml_dtypes.bfloat16)
    low = (table - high.astype(np.float64)).astype(ml_dtypes.bfloat16)
    eye = np.eye(GROUP)
    return [np.kron(part.astype(np.float64), eye).astype(ml_dtypes.bfloat16) for part in (high, low)]


def roll(values, shift):
    return pltpu.roll(values.astype(jnp.float32), shift, 1).astype(values.dtype)


def product_kernel(occ_ref, virt_ref, out_ref, occ, virt, out, in_sems, out_sems):
    n_dest = out_ref.shape[0]
    n_time, rows, _ = occ.shape
    blocks = [(t, pl.ds(start, GROUP)) for t in range(n_time) for start in range(0, rows, GROUP)]
    loads, stores = [], []
    for q, (t, block) in enumerate(blocks):
        pair = [
            pltpu.make_async_copy(src.at[t, block], dst.at[t, block], in_sems.at[q, s])
            for s, (src, dst) in enumerate(((occ_ref, occ), (virt_ref, virt)))
        ]
        for load in pair:
            load.start()
        loads.append(pair)

    def send(part, first, count):
        rows = pl.ds(first * GROUP, count * GROUP)
        store = pltpu.make_async_copy(out.at[:, rows], out_ref.at[:, rows], out_sems.at[part])
        store.start()
        stores.append(store)

    quarter = lax.broadcasted_iota(jnp.int32, (GROUP, LANES), 1) // SHIFT
    rests = {}
    for q, (t, block) in enumerate(blocks):
        for load in loads[q]:
            load.wait()

        def tile(k):
            columns = pl.ds(k * LANES, LANES)
            return occ[t, block, columns] * virt[t, block, columns]

        for j in range(n_dest):
            start = j * (FULL * QUARTERS + QUARTERS - 1)
            head = -start % QUARTERS
            hole = QUARTERS - 1 - head
            first = (start + head) // QUARTERS
            for m in range(FULL):
                out[j, pl.ds((q * FULL + m) * GROUP, GROUP), :] = tile(first + m)
            if head == 0:
                rest = tile(first + FULL)
            elif hole == 0:
                rest = tile(first - 1)
            else:
                rest = jnp.where(quarter > hole, tile(first - 1), tile(first + FULL))
            rests[j, q] = rest
        if q < len(blocks) - 1:
            send(q, q * FULL, FULL)
            continue
        for j in range(n_dest):
            hole = QUARTERS - 1 - -j * (FULL * QUARTERS + QUARTERS - 1) % QUARTERS
            for m in range(FULL):
                moved = roll(rests[j, q], LANES - (1 + m) * SHIFT)
                filled = jnp.where(quarter == hole, moved, rests[j, m])
                out[j, pl.ds(((q + 1) * FULL + m) * GROUP, GROUP), :] = filled
        send(q, q * FULL, 2 * FULL)
    for store in stores:
        store.wait()


def own_place():
    head = lax.rem(lax.axis_index("tm"), QUARTERS)
    return head, QUARTERS - 1 - head


def transformed(high_ref, low_ref, values):
    total = jnp.dot(high_ref[...], values, preferred_element_type=jnp.float32)
    return total + jnp.dot(low_ref[...], values, preferred_element_type=jnp.float32)


def adjoint_kernel(high_ref, low_ref, adjoint_ref, out_ref):
    n_freq, rows, width = adjoint_ref.shape
    n_source = out_ref.shape[0]
    per_source, halves = n_freq // n_source, rows // GROUP
    n_block = per_source * halves
    head, hole = own_place()
    split = LANES - head * SHIFT
    quarter = lax.broadcasted_iota(jnp.int32, (GROUP, LANES), 1) // SHIFT
    wide = lax.broadcasted_iota(jnp.int32, (n_freq * GROUP, LANES), 1)
    rests = {}
    for half in range(halves):
        block = pl.ds(half * GROUP, GROUP)
        values = adjoint_ref[:, block, :].reshape(n_freq * GROUP, width)
        total = transformed(high_ref, low_ref, values)
        pad = jnp.zeros((n_freq * GROUP, (FULL + 1) * LANES - width), jnp.float32)
        total = jnp.concatenate([total, pad], axis=1)
        turned = [
            pltpu.roll(total[:, m * LANES : (m + 1) * LANES], lax.rem(split, LANES), 1)
            for m in range(FULL + 1)
        ]
        packed = [jnp.where(wide < split, turned[m], turned[m + 1]) for m in range(FULL)]
        rest = jnp.where(wide < split, turned[FULL], turned[0])
        for t in range(n_freq):
            i, tt = divmod(t, per_source)
            q = tt * halves + half
            lines = slice(t * GROUP, (t + 1) * GROUP)
            for m in range(FULL):
                out_ref[i, pl.ds((q * FULL + m) * GROUP, GROUP), :] = packed[m][lines]
            rests[i, q] = rest[lines]
    for i in range(n_source):
        for m in range(FULL):
            moved = pltpu.roll(rests[i, n_block - 1], LANES - (1 + m) * SHIFT, 1)
            filled = jnp.where(quarter == hole, moved, rests[i, m])
            out_ref[i, pl.ds((n_block * FULL + m) * GROUP, GROUP), :] = filled


def energy_kernel(rows, times_ref, adjoint_ref, weight_ref, label_ref, message_ref):
    n_source, lines, _ = times_ref.shape
    n_block = lines // GROUP // FULL - 1
    halves = rows // GROUP
    _, hole = own_place()
    in_hole = lax.broadcasted_iota(jnp.int32, (GROUP, LANES), 1) // SHIFT == hole
    sums = [jnp.zeros((GROUP, LANES), jnp.float32) for _ in range(halves)]

    def terms(tile):
        lines = pl.ds(tile * GROUP, GROUP)
        total = jnp.zeros((GROUP, LANES), jnp.float32)
        for i in range(n_source):
            total += times_ref[i, lines, :].astype(jnp.float32) * adjoint_ref[i, lines, :]
        return total

    for q in range(n_block):
        for m in range(FULL):
            sums[q % halves] += terms(q * FULL + m)
    for m in range(FULL):
        rest = terms(n_block * FULL + m)
        sums[m % halves] += jnp.where(in_hole, 0.0, rest)
        sums[(n_block - 1) % halves] += jnp.where(in_hole, rest, 0.0)
    total = jnp.zeros((1, LANES), jnp.float32)
    for half in range(halves):
        energy = jnp.sum(sums[half], axis=1, keepdims=True)
        row = lax.broadcasted_iota(jnp.int32, (GROUP, LANES), 0) + half * GROUP
        lane = lax.broadcasted_iota(jnp.int32, (GROUP, LANES), 1)
        total += jnp.sum(jnp.where(lane % rows == row, energy, 0.0), axis=0, keepdims=True)
    message = total * weight_ref[...] + label_ref[...]
    message_ref[...] = jnp.broadcast_to(message, message_ref.shape)


def chi_kernel(high_ref, low_ref, times_ref, chi_ref):
    n_source = times_ref.shape[0]
    n_freq, rows, width = chi_ref.shape
    head, hole = own_place()
    turn = head * SHIFT
    quarter = lax.broadcasted_iota(jnp.int32, (GROUP, LANES), 1) // SHIFT
    wide = lax.broadcasted_iota(jnp.int32, (n_freq * GROUP, LANES), 1)
    n_block = NTAU // n_source * (rows // GROUP)

    def stored(i, tile):
        return times_ref[i, pl.ds(tile * GROUP, GROUP), :]

    def last_rest(i):
        rest = stored(i, n_block * FULL)
        for m in range(FULL):
            moved = roll(stored(i, n_block * FULL + m), (1 + m) * SHIFT)
            rest = jnp.where(quarter == lax.rem(hole + 1 + m, QUARTERS), moved, rest)
        return rest

    def column_tile(half, m):
        parts = []
        for t in range(NTAU):
            i, tt = divmod(t, NTAU // n_source)
            q = tt * (rows // GROUP) + half
            if m < FULL:
                parts.append(stored(i, q * FULL + m))
            elif q < n_block - 1:
                parts.append(stored(i, n_block * FULL + q))
            else:
                parts.append(last_rest(i))
        return jnp.concatenate(parts, axis=0)

    for half in range(rows // GROUP):
        block = pl.ds(half * GROUP, GROUP)
        values = jnp.concatenate([column_tile(half, m) for m in range(FULL + 1)], axis=1)
        chi = transformed(high_ref, low_ref, values)
        turned = [pltpu.roll(chi[:, m * LANES : (m + 1) * LANES], turn, 1) for m in range(FULL + 1)]
        for m in range(FULL + 1):
            count = min(LANES, width - m * LANES)
            natural = jnp.where(wide < turn, turned[m - 1], turned[m])[:, :count]
            natural = natural.astype(jnp.bfloat16).reshape(n_freq, GROUP, count)
            chi_ref[:, block, pl.ds(m * LANES, count)] = natural


def forces_kernel(rows, n_col, message_ref, forces_ref):
    sums = []
    for block in range(message_ref.shape[0] // n_col * CORES):
        pair, core = divmod(block, CORES)
        devices = pl.ds(pair * n_col, n_col)
        sums.append(jnp.sum(message_ref[devices, core, :], axis=0, keepdims=True))
    parts = [
        jnp.concatenate([total[:, p * rows : (p + 1) * rows] for total in sums], axis=1)
        for p in range(4)
    ]
    owners = parts[3].astype(jnp.int32)
    weights = jnp.concatenate(parts[:3] + [jnp.zeros_like(parts[0])] * 5, axis=0)
    upper, lower = owners // LANES, owners % LANES
    n_upper = pl.cdiv(NATOM, LANES)
    rest = jnp.concatenate([jnp.where(upper == u, weights, 0.0) for u in range(n_upper)], axis=0)
    lanes = lax.broadcasted_iota(jnp.int32, (LANES, owners.shape[1]), 0)
    onehot = jnp.where(lanes == lower, 1.0, 0.0).astype(jnp.bfloat16)
    forces = jnp.zeros((8 * n_upper, LANES), jnp.float32)
    for _ in range(3):
        part = rest.astype(jnp.bfloat16)
        rest = rest - part.astype(jnp.float32)
        forces += lax.dot_general(
            part, onehot, (((1,), (1,)), ((), ())), preferred_element_type=jnp.float32
        )
    for u in range(n_upper):
        count = min(LANES, NATOM - u * LANES)
        forces_ref[:, u * LANES : u * LANES + count] = forces[u * 8 : u * 8 + 3, :count]


def on_device(sizes, green_occ, green_virt, adjoint_w, grad_basis, owner_map, block_offset):
    n_pair, n_col, n_tm = sizes
    n_time, rows, columns = green_occ.shape
    width = columns // n_tm
    high, low = (jnp.asarray(part) for part in transform_matrix())
    n_block = n_time * rows // GROUP
    tiles = n_block * FULL + FULL
    assert width == FULL * LANES + (QUARTERS - 1) * SHIFT and n_block == FULL + 1

    packed = (n_tm, tiles * GROUP, LANES)
    product = pl.pallas_call(
        product_kernel,
        in_specs=[pl.BlockSpec(memory_space=pl.ANY)] * 2,
        out_specs=pl.BlockSpec(memory_space=pl.ANY),
        out_shape=jax.ShapeDtypeStruct(packed, jnp.bfloat16),
        scratch_shapes=[
            pltpu.VMEM(green_occ.shape, jnp.bfloat16),
            pltpu.VMEM(green_virt.shape, jnp.bfloat16),
            pltpu.VMEM(packed, jnp.bfloat16),
            pltpu.SemaphoreType.DMA((n_block, 2)),
            pltpu.SemaphoreType.DMA((n_block,)),
        ],
        compiler_params=pltpu.CompilerParams(vmem_limit_bytes=60 << 20),
        name="product",
    )(green_occ, green_virt)
    times = lax.all_to_all(product, "tm", split_axis=0, concat_axis=0, tiled=True)

    def kernel(body, name, shape, dtype, limit, *operands):
        elements = NTAU * rows * width
        return pl.pallas_call(
            body,
            out_shape=jax.ShapeDtypeStruct(shape, dtype),
            cost_estimate=pl.CostEstimate(
                flops=4 * NTAU * GROUP * elements, bytes_accessed=4 * elements, transcendentals=0
            ),
            compiler_params=pltpu.CompilerParams(vmem_limit_bytes=limit << 20),
            name=name,
        )(*operands)

    scale = 1.0 / math.sqrt(NTAU * NG)
    owners = lax.dynamic_slice_in_dim(owner_map, block_offset[0], rows, 0)
    weight = jnp.concatenate([grad_basis.reshape(3 * rows) * scale, jnp.zeros((rows,), jnp.float32)])
    label = jnp.concatenate(
        [jnp.zeros((3 * rows,), jnp.float32), owners.astype(jnp.float32) * (1.0 / (n_col * n_tm))]
    )
    adjoint = kernel(adjoint_kernel, "adjoint", packed, jnp.float32, 16, high, low, adjoint_w)
    message = pl.pallas_call(
        functools.partial(energy_kernel, rows),
        out_shape=jax.ShapeDtypeStruct((CORES * n_tm, LANES), jnp.float32),
        compiler_params=pltpu.CompilerParams(vmem_limit_bytes=16 << 20),
        name="energy",
    )(times, adjoint, weight[None, :], label[None, :])

    message = lax.all_to_all(message, ("core", "tm"), split_axis=0, concat_axis=0, tiled=True)
    chi_freq = kernel(
        chi_kernel, "chi_freq", (NTAU, rows, width), jnp.bfloat16, 16, high, low, times
    )
    message = jnp.sum(message.reshape(CORES, n_tm, LANES), axis=1)
    message = jnp.broadcast_to(message[None], (n_pair * n_col, CORES, LANES))
    message = lax.all_to_all(message, ("pair", "col"), split_axis=0, concat_axis=0, tiled=True)
    forces = pl.pallas_call(
        functools.partial(forces_kernel, rows, n_col),
        out_shape=jax.ShapeDtypeStruct((3, NATOM), jnp.float32),
        compiler_params=pltpu.CompilerParams(vmem_limit_bytes=8 << 20),
        name="forces",
    )(message)
    return (chi_freq, forces)


def solution(mesh):
    n_row, n_col, n_tm = (mesh.shape[name] for name in ("row", "col", "tm"))
    n_pair = n_row // CORES
    fine = Mesh(mesh.devices.reshape(n_pair, CORES, n_col, n_tm), ("pair", "core", "col", "tm"))
    row = ("pair", "core")
    in_specs = (
        P("tm", row, "col"),
        P("tm", row, "col"),
        P(None, row, ("col", "tm")),
        P(None, row),
        P(),
        P(row),
    )
    out_specs = (P(None, row, ("col", "tm")), P())
    return jax.shard_map(
        functools.partial(on_device, (n_pair, n_col, n_tm)),
        mesh=fine,
        in_specs=in_specs,
        out_specs=out_specs,
        check_vma=False,
    )
```

```python
import functools
import math

import jax
import jax.numpy as jnp
import ml_dtypes
import numpy as np
from jax import lax
from jax.experimental import pallas as pl
from jax.experimental.pallas import tpu as pltpu
from jax.sharding import Mesh, PartitionSpec as P

NG = 30720
NTAU = 16
NATOM = 1000
GROUP = 16
LANES = 128
SHIFT = 32
QUARTERS = LANES // SHIFT
FULL = 3
CORES = 2
FAR = 2


def transform_matrix():
    steps = np.arange(NTAU, dtype=np.float64)
    table = np.cos(0.1 * 0.15 * 1.35 ** (steps[:, None] + steps[None, :])) / 4.0
    high = table.astype(ml_dtypes.bfloat16)
    low = (table - high.astype(np.float64)).astype(ml_dtypes.bfloat16)
    eye = np.eye(GROUP)
    return [np.kron(part.astype(np.float64), eye).astype(ml_dtypes.bfloat16) for part in (high, low)]


def roll(values, shift):
    return pltpu.roll(values.astype(jnp.float32), shift, 1).astype(values.dtype)


def product_kernel(occ_ref, virt_ref, out_ref, occ, virt, out, in_sems, out_sems):
    n_dest = out_ref.shape[0]
    n_time, rows, _ = occ.shape
    blocks = [(t, pl.ds(start, GROUP)) for t in range(n_time) for start in range(0, rows, GROUP)]
    loads, stores = [], []
    for q, (t, block) in enumerate(blocks):
        pair = [
            pltpu.make_async_copy(src.at[t, block], dst.at[t, block], in_sems.at[q, s])
            for s, (src, dst) in enumerate(((occ_ref, occ), (virt_ref, virt)))
        ]
        for load in pair:
            load.start()
        loads.append(pair)

    def send(part, first, count):
        rows = pl.ds(first * GROUP, count * GROUP)
        store = pltpu.make_async_copy(out.at[:, rows], out_ref.at[:, rows], out_sems.at[part])
        store.start()
        stores.append(store)

    quarter = lax.broadcasted_iota(jnp.int32, (GROUP, LANES), 1) // SHIFT
    rests = {}
    for q, (t, block) in enumerate(blocks):
        for load in loads[q]:
            load.wait()

        def tile(k):
            columns = pl.ds(k * LANES, LANES)
            return occ[t, block, columns] * virt[t, block, columns]

        for j in range(n_dest):
            start = j * (FULL * QUARTERS + QUARTERS - 1)
            head = -start % QUARTERS
            hole = QUARTERS - 1 - head
            first = (start + head) // QUARTERS
            for m in range(FULL):
                out[j, pl.ds((q * FULL + m) * GROUP, GROUP), :] = tile(first + m)
            if head == 0:
                rest = tile(first + FULL)
            elif hole == 0:
                rest = tile(first - 1)
            else:
                rest = jnp.where(quarter > hole, tile(first - 1), tile(first + FULL))
            rests[j, q] = rest
        if q < len(blocks) - 1:
            send(q, q * FULL, FULL)
            continue
        for j in range(n_dest):
            hole = QUARTERS - 1 - -j * (FULL * QUARTERS + QUARTERS - 1) % QUARTERS
            for m in range(FULL):
                moved = roll(rests[j, q], LANES - (1 + m) * SHIFT)
                filled = jnp.where(quarter == hole, moved, rests[j, m])
                out[j, pl.ds(((q + 1) * FULL + m) * GROUP, GROUP), :] = filled
        send(q, q * FULL, 2 * FULL)
    for store in stores:
        store.wait()


def own_place():
    head = lax.rem(lax.axis_index("tm"), QUARTERS)
    return head, QUARTERS - 1 - head


def transformed(high_ref, low_ref, values):
    total = jnp.dot(high_ref[...], values, preferred_element_type=jnp.float32)
    return total + jnp.dot(low_ref[...], values, preferred_element_type=jnp.float32)


def adjoint_kernel(high_ref, low_ref, adjoint_ref, out_ref):
    n_freq, rows, width = adjoint_ref.shape
    n_source = out_ref.shape[0]
    per_source, halves = n_freq // n_source, rows // GROUP
    n_block = per_source * halves
    head, hole = own_place()
    split = LANES - head * SHIFT
    quarter = lax.broadcasted_iota(jnp.int32, (GROUP, LANES), 1) // SHIFT
    wide = lax.broadcasted_iota(jnp.int32, (n_freq * GROUP, LANES), 1)
    rests = {}
    for half in range(halves):
        block = pl.ds(half * GROUP, GROUP)
        values = adjoint_ref[:, block, :].reshape(n_freq * GROUP, width)
        total = transformed(high_ref, low_ref, values)
        pad = jnp.zeros((n_freq * GROUP, (FULL + 1) * LANES - width), jnp.float32)
        total = jnp.concatenate([total, pad], axis=1)
        turned = [
            pltpu.roll(total[:, m * LANES : (m + 1) * LANES], lax.rem(split, LANES), 1)
            for m in range(FULL + 1)
        ]
        packed = [jnp.where(wide < split, turned[m], turned[m + 1]) for m in range(FULL)]
        rest = jnp.where(wide < split, turned[FULL], turned[0])
        for t in range(n_freq):
            i, tt = divmod(t, per_source)
            q = tt * halves + half
            lines = slice(t * GROUP, (t + 1) * GROUP)
            for m in range(FULL):
                out_ref[i, pl.ds((q * FULL + m) * GROUP, GROUP), :] = packed[m][lines]
            rests[i, q] = rest[lines]
    for i in range(n_source):
        for m in range(FULL):
            moved = pltpu.roll(rests[i, n_block - 1], LANES - (1 + m) * SHIFT, 1)
            filled = jnp.where(quarter == hole, moved, rests[i, m])
            out_ref[i, pl.ds((n_block * FULL + m) * GROUP, GROUP), :] = filled


def energy_kernel(rows, times_ref, adjoint_ref, weight_ref, label_ref, message_ref):
    n_source, lines, _ = times_ref.shape
    n_block = lines // GROUP // FULL - 1
    halves = rows // GROUP
    _, hole = own_place()
    in_hole = lax.broadcasted_iota(jnp.int32, (GROUP, LANES), 1) // SHIFT == hole
    sums = [jnp.zeros((GROUP, LANES), jnp.float32) for _ in range(halves)]

    def terms(tile):
        lines = pl.ds(tile * GROUP, GROUP)
        total = jnp.zeros((GROUP, LANES), jnp.float32)
        for i in range(n_source):
            total += times_ref[i, lines, :].astype(jnp.float32) * adjoint_ref[i, lines, :]
        return total

    for q in range(n_block):
        for m in range(FULL):
            sums[q % halves] += terms(q * FULL + m)
    for m in range(FULL):
        rest = terms(n_block * FULL + m)
        sums[m % halves] += jnp.where(in_hole, 0.0, rest)
        sums[(n_block - 1) % halves] += jnp.where(in_hole, rest, 0.0)
    total = jnp.zeros((1, LANES), jnp.float32)
    for half in range(halves):
        energy = jnp.sum(sums[half], axis=1, keepdims=True)
        row = lax.broadcasted_iota(jnp.int32, (GROUP, LANES), 0) + half * GROUP
        lane = lax.broadcasted_iota(jnp.int32, (GROUP, LANES), 1)
        total += jnp.sum(jnp.where(lane % rows == row, energy, 0.0), axis=0, keepdims=True)
    message = total * weight_ref[...] + label_ref[...]
    message_ref[...] = jnp.broadcast_to(message, message_ref.shape)


def chi_kernel(high_ref, low_ref, times_ref, chi_ref):
    n_source = times_ref.shape[0]
    n_freq, rows, width = chi_ref.shape
    head, hole = own_place()
    turn = head * SHIFT
    quarter = lax.broadcasted_iota(jnp.int32, (GROUP, LANES), 1) // SHIFT
    wide = lax.broadcasted_iota(jnp.int32, (n_freq * GROUP, LANES), 1)
    n_block = NTAU // n_source * (rows // GROUP)

    def stored(i, tile):
        return times_ref[i, pl.ds(tile * GROUP, GROUP), :]

    def last_rest(i):
        rest = stored(i, n_block * FULL)
        for m in range(FULL):
            moved = roll(stored(i, n_block * FULL + m), (1 + m) * SHIFT)
            rest = jnp.where(quarter == lax.rem(hole + 1 + m, QUARTERS), moved, rest)
        return rest

    def column_tile(half, m):
        parts = []
        for t in range(NTAU):
            i, tt = divmod(t, NTAU // n_source)
            q = tt * (rows // GROUP) + half
            if m < FULL:
                parts.append(stored(i, q * FULL + m))
            elif q < n_block - 1:
                parts.append(stored(i, n_block * FULL + q))
            else:
                parts.append(last_rest(i))
        return jnp.concatenate(parts, axis=0)

    for half in range(rows // GROUP):
        block = pl.ds(half * GROUP, GROUP)
        values = jnp.concatenate([column_tile(half, m) for m in range(FULL + 1)], axis=1)
        chi = transformed(high_ref, low_ref, values)
        turned = [pltpu.roll(chi[:, m * LANES : (m + 1) * LANES], turn, 1) for m in range(FULL + 1)]
        for m in range(FULL + 1):
            count = min(LANES, width - m * LANES)
            natural = jnp.where(wide < turn, turned[m - 1], turned[m])[:, :count]
            natural = natural.astype(jnp.bfloat16).reshape(n_freq, GROUP, count)
            chi_ref[:, block, pl.ds(m * LANES, count)] = natural


def forces_kernel(rows, n_col, message_ref, forces_ref):
    sums = []
    for block in range(message_ref.shape[0] // n_col * CORES):
        pair, core = divmod(block, CORES)
        devices = pl.ds(pair * n_col, n_col)
        sums.append(jnp.sum(message_ref[devices, core, :], axis=0, keepdims=True))
    parts = [
        jnp.concatenate([total[:, p * rows : (p + 1) * rows] for total in sums], axis=1)
        for p in range(4)
    ]
    owners = parts[3].astype(jnp.int32)
    weights = jnp.concatenate(parts[:3] + [jnp.zeros_like(parts[0])] * 5, axis=0)
    upper, lower = owners // LANES, owners % LANES
    n_upper = pl.cdiv(NATOM, LANES)
    rest = jnp.concatenate([jnp.where(upper == u, weights, 0.0) for u in range(n_upper)], axis=0)
    lanes = lax.broadcasted_iota(jnp.int32, (LANES, owners.shape[1]), 0)
    onehot = jnp.where(lanes == lower, 1.0, 0.0).astype(jnp.bfloat16)
    forces = jnp.zeros((8 * n_upper, LANES), jnp.float32)
    for _ in range(3):
        part = rest.astype(jnp.bfloat16)
        rest = rest - part.astype(jnp.float32)
        forces += lax.dot_general(
            part, onehot, (((1,), (1,)), ((), ())), preferred_element_type=jnp.float32
        )
    for u in range(n_upper):
        count = min(LANES, NATOM - u * LANES)
        forces_ref[:, u * LANES : u * LANES + count] = forces[u * 8 : u * 8 + 3, :count]


def on_device(sizes, green_occ, green_virt, adjoint_w, grad_basis, owner_map, block_offset):
    n_pair, n_near, n_tm = sizes
    n_col = n_near * FAR
    n_time, rows, columns = green_occ.shape
    width = columns // n_tm
    high, low = (jnp.asarray(part) for part in transform_matrix())
    n_block = n_time * rows // GROUP
    tiles = n_block * FULL + FULL
    assert width == FULL * LANES + (QUARTERS - 1) * SHIFT and n_block == FULL + 1

    packed = (n_tm, tiles * GROUP, LANES)
    product = pl.pallas_call(
        product_kernel,
        in_specs=[pl.BlockSpec(memory_space=pl.ANY)] * 2,
        out_specs=pl.BlockSpec(memory_space=pl.ANY),
        out_shape=jax.ShapeDtypeStruct(packed, jnp.bfloat16),
        scratch_shapes=[
            pltpu.VMEM(green_occ.shape, jnp.bfloat16),
            pltpu.VMEM(green_virt.shape, jnp.bfloat16),
            pltpu.VMEM(packed, jnp.bfloat16),
            pltpu.SemaphoreType.DMA((n_block, 2)),
            pltpu.SemaphoreType.DMA((n_block,)),
        ],
        compiler_params=pltpu.CompilerParams(vmem_limit_bytes=60 << 20),
        name="product",
    )(green_occ, green_virt)
    times = lax.all_to_all(product, "tm", split_axis=0, concat_axis=0, tiled=True)

    def kernel(body, name, shape, dtype, limit, *operands):
        elements = NTAU * rows * width
        return pl.pallas_call(
            body,
            out_shape=jax.ShapeDtypeStruct(shape, dtype),
            cost_estimate=pl.CostEstimate(
                flops=4 * NTAU * GROUP * elements, bytes_accessed=4 * elements, transcendentals=0
            ),
            compiler_params=pltpu.CompilerParams(vmem_limit_bytes=limit << 20),
            name=name,
        )(*operands)

    scale = 1.0 / math.sqrt(NTAU * NG)
    owners = lax.dynamic_slice_in_dim(owner_map, block_offset[0], rows, 0)
    weight = jnp.concatenate([grad_basis.reshape(3 * rows) * scale, jnp.zeros((rows,), jnp.float32)])
    label = jnp.concatenate(
        [jnp.zeros((3 * rows,), jnp.float32), owners.astype(jnp.float32) * (1.0 / (n_col * n_tm))]
    )
    adjoint = kernel(adjoint_kernel, "adjoint", packed, jnp.float32, 16, high, low, adjoint_w)
    message = pl.pallas_call(
        functools.partial(energy_kernel, rows),
        out_shape=jax.ShapeDtypeStruct((CORES * n_near * n_tm, LANES), jnp.float32),
        compiler_params=pltpu.CompilerParams(vmem_limit_bytes=16 << 20),
        name="energy",
    )(times, adjoint, weight[None, :], label[None, :])

    message = lax.all_to_all(message, ("core", "near", "tm"), split_axis=0, concat_axis=0, tiled=True)
    chi_freq = kernel(
        chi_kernel, "chi_freq", (NTAU, rows, width), jnp.bfloat16, 16, high, low, times
    )
    message = jnp.sum(message.reshape(CORES, n_near * n_tm, LANES), axis=1)
    message = jnp.broadcast_to(message[None], (n_pair * FAR, CORES, LANES))
    message = lax.all_to_all(message, ("pair", "far"), split_axis=0, concat_axis=0, tiled=True)
    forces = pl.pallas_call(
        functools.partial(forces_kernel, rows, FAR),
        out_shape=jax.ShapeDtypeStruct((3, NATOM), jnp.float32),
        compiler_params=pltpu.CompilerParams(vmem_limit_bytes=8 << 20),
        name="forces",
    )(message)
    return (chi_freq, forces)


def solution(mesh):
    n_row, n_col, n_tm = (mesh.shape[name] for name in ("row", "col", "tm"))
    n_pair = n_row // CORES
    n_near = n_col // FAR
    axes = ("pair", "core", "near", "far", "tm")
    fine = Mesh(mesh.devices.reshape(n_pair, CORES, n_near, FAR, n_tm), axes)
    row, col = ("pair", "core"), ("near", "far")
    in_specs = (
        P("tm", row, col),
        P("tm", row, col),
        P(None, row, col + ("tm",)),
        P(None, row),
        P(),
        P(row),
    )
    out_specs = (P(None, row, col + ("tm",)), P())
    return jax.shard_map(
        functools.partial(on_device, (n_pair, n_near, n_tm)),
        mesh=fine,
        in_specs=in_specs,
        out_specs=out_specs,
        check_vma=False,
    )
```

```python
import functools
import math

import jax
import jax.numpy as jnp
import ml_dtypes
import numpy as np
from jax import lax
from jax.experimental import pallas as pl
from jax.experimental.pallas import tpu as pltpu
from jax.sharding import Mesh, PartitionSpec as P

NG = 30720
NTAU = 16
NATOM = 1000
GROUP = 16
LANES = 128
SHIFT = 32
QUARTERS = LANES // SHIFT
FULL = 3
CORES = 2
FAR = 2


def transform_matrix():
    steps = np.arange(NTAU, dtype=np.float64)
    table = np.cos(0.1 * 0.15 * 1.35 ** (steps[:, None] + steps[None, :])) / 4.0
    high = table.astype(ml_dtypes.bfloat16)
    low = (table - high.astype(np.float64)).astype(ml_dtypes.bfloat16)
    eye = np.eye(GROUP)
    return [np.kron(part.astype(np.float64), eye).astype(ml_dtypes.bfloat16) for part in (high, low)]


def roll(values, shift):
    return pltpu.roll(values.astype(jnp.float32), shift, 1).astype(values.dtype)


def product_kernel(occ_ref, virt_ref, out_ref, occ, virt, out, in_sems, out_sems):
    n_dest = out_ref.shape[0]
    n_time, rows, _ = occ.shape
    blocks = [(t, pl.ds(start, GROUP)) for t in range(n_time) for start in range(0, rows, GROUP)]
    loads, stores = [], []
    for q, (t, block) in enumerate(blocks):
        pair = [
            pltpu.make_async_copy(src.at[t, block], dst.at[t, block], in_sems.at[q, s])
            for s, (src, dst) in enumerate(((occ_ref, occ), (virt_ref, virt)))
        ]
        for load in pair:
            load.start()
        loads.append(pair)

    def send(part, first, count):
        rows = pl.ds(first * GROUP, count * GROUP)
        store = pltpu.make_async_copy(out.at[:, rows], out_ref.at[:, rows], out_sems.at[part])
        store.start()
        stores.append(store)

    quarter = lax.broadcasted_iota(jnp.int32, (GROUP, LANES), 1) // SHIFT
    rests = {}
    for q, (t, block) in enumerate(blocks):
        for load in loads[q]:
            load.wait()

        def tile(k):
            columns = pl.ds(k * LANES, LANES)
            return occ[t, block, columns] * virt[t, block, columns]

        for j in range(n_dest):
            start = j * (FULL * QUARTERS + QUARTERS - 1)
            head = -start % QUARTERS
            hole = QUARTERS - 1 - head
            first = (start + head) // QUARTERS
            for m in range(FULL):
                out[j, pl.ds((q * FULL + m) * GROUP, GROUP), :] = tile(first + m)
            if head == 0:
                rest = tile(first + FULL)
            elif hole == 0:
                rest = tile(first - 1)
            else:
                rest = jnp.where(quarter > hole, tile(first - 1), tile(first + FULL))
            rests[j, q] = rest
        if q < len(blocks) - 1:
            send(q, q * FULL, FULL)
            continue
        for j in range(n_dest):
            hole = QUARTERS - 1 - -j * (FULL * QUARTERS + QUARTERS - 1) % QUARTERS
            for m in range(FULL):
                moved = roll(rests[j, q], LANES - (1 + m) * SHIFT)
                filled = jnp.where(quarter == hole, moved, rests[j, m])
                out[j, pl.ds(((q + 1) * FULL + m) * GROUP, GROUP), :] = filled
        send(q, q * FULL, 2 * FULL)
    for store in stores:
        store.wait()


def own_place():
    head = lax.rem(lax.axis_index("tm"), QUARTERS)
    return head, QUARTERS - 1 - head


def transformed(high_ref, low_ref, values):
    total = jnp.dot(high_ref[...], values, preferred_element_type=jnp.float32)
    return total + jnp.dot(low_ref[...], values, preferred_element_type=jnp.float32)


def transform_kernel(
    high_ref, low_ref, times_ref, adjoint_ref, weight_ref, label_ref, chi_ref, message_ref
):
    n_source = times_ref.shape[0]
    n_freq, rows, width = chi_ref.shape
    head, hole = own_place()
    turn = head * SHIFT
    quarter = lax.broadcasted_iota(jnp.int32, (GROUP, LANES), 1) // SHIFT
    wide = lax.broadcasted_iota(jnp.int32, (n_freq * GROUP, LANES), 1)
    n_block = NTAU // n_source * (rows // GROUP)

    def stored(i, tile):
        return times_ref[i, pl.ds(tile * GROUP, GROUP), :]

    def last_rest(i):
        rest = stored(i, n_block * FULL)
        for m in range(FULL):
            moved = roll(stored(i, n_block * FULL + m), (1 + m) * SHIFT)
            rest = jnp.where(quarter == lax.rem(hole + 1 + m, QUARTERS), moved, rest)
        return rest

    def column_tile(half, m):
        parts = []
        for t in range(NTAU):
            i, tt = divmod(t, NTAU // n_source)
            q = tt * (rows // GROUP) + half
            if m < FULL:
                parts.append(stored(i, q * FULL + m))
            elif q < n_block - 1:
                parts.append(stored(i, n_block * FULL + q))
            else:
                parts.append(last_rest(i))
        return jnp.concatenate(parts, axis=0)

    total = jnp.zeros((1, LANES), jnp.float32)
    for half in range(rows // GROUP):
        block = pl.ds(half * GROUP, GROUP)
        values = jnp.concatenate([column_tile(half, m) for m in range(FULL + 1)], axis=1)
        chi = transformed(high_ref, low_ref, values)
        turned = [pltpu.roll(chi[:, m * LANES : (m + 1) * LANES], turn, 1) for m in range(FULL + 1)]
        energy = jnp.zeros((GROUP, 1), jnp.float32)
        for m in range(FULL + 1):
            before = turned[m - 1]
            count = min(LANES, width - m * LANES)
            columns = pl.ds(m * LANES, count)
            natural = jnp.where(wide < turn, before, turned[m])[:, :count].astype(jnp.bfloat16)
            natural = natural.reshape(n_freq, GROUP, count)
            chi_ref[:, block, columns] = natural
            terms = adjoint_ref[:, block, columns].astype(jnp.float32) * natural.astype(jnp.float32)
            energy += jnp.sum(jnp.sum(terms, axis=0), axis=1, keepdims=True)
        row = lax.broadcasted_iota(jnp.int32, (GROUP, LANES), 0) + half * GROUP
        lane = lax.broadcasted_iota(jnp.int32, (GROUP, LANES), 1)
        total += jnp.sum(jnp.where(lane % rows == row, energy, 0.0), axis=0, keepdims=True)
    message = total * weight_ref[...] + label_ref[...]
    message_ref[...] = jnp.broadcast_to(message, message_ref.shape)


def forces_kernel(rows, n_col, message_ref, chi_ref, forces_out_ref, chi_out_ref, forces_ref, sems):
    store = pltpu.make_async_copy(chi_ref, chi_out_ref, sems.at[0])
    store.start()
    sums = []
    for block in range(message_ref.shape[0] // n_col * CORES):
        pair, core = divmod(block, CORES)
        devices = pl.ds(pair * n_col, n_col)
        sums.append(jnp.sum(message_ref[devices, core, :], axis=0, keepdims=True))
    parts = [
        jnp.concatenate([total[:, p * rows : (p + 1) * rows] for total in sums], axis=1)
        for p in range(4)
    ]
    owners = parts[3].astype(jnp.int32)
    weights = jnp.concatenate(parts[:3] + [jnp.zeros_like(parts[0])] * 5, axis=0)
    upper, lower = owners // LANES, owners % LANES
    n_upper = pl.cdiv(NATOM, LANES)
    rest = jnp.concatenate([jnp.where(upper == u, weights, 0.0) for u in range(n_upper)], axis=0)
    lanes = lax.broadcasted_iota(jnp.int32, (LANES, owners.shape[1]), 0)
    onehot = jnp.where(lanes == lower, 1.0, 0.0).astype(jnp.bfloat16)
    forces = jnp.zeros((8 * n_upper, LANES), jnp.float32)
    for _ in range(3):
        part = rest.astype(jnp.bfloat16)
        rest = rest - part.astype(jnp.float32)
        forces += lax.dot_general(
            part, onehot, (((1,), (1,)), ((), ())), preferred_element_type=jnp.float32
        )
    for u in range(n_upper):
        count = min(LANES, NATOM - u * LANES)
        forces_ref[:, u * LANES : u * LANES + count] = forces[u * 8 : u * 8 + 3, :count]
    forces_store = pltpu.make_async_copy(forces_ref, forces_out_ref, sems.at[1])
    forces_store.start()
    forces_store.wait()
    store.wait()


def on_device(sizes, green_occ, green_virt, adjoint_w, grad_basis, owner_map, block_offset):
    n_pair, n_near, n_tm = sizes
    n_col = n_near * FAR
    n_time, rows, columns = green_occ.shape
    width = columns // n_tm
    high, low = (jnp.asarray(part) for part in transform_matrix())
    n_block = n_time * rows // GROUP
    tiles = n_block * FULL + FULL
    assert width == FULL * LANES + (QUARTERS - 1) * SHIFT and n_block == FULL + 1

    packed = (n_tm, tiles * GROUP, LANES)
    product = pl.pallas_call(
        product_kernel,
        in_specs=[pl.BlockSpec(memory_space=pl.ANY)] * 2,
        out_specs=pl.BlockSpec(memory_space=pl.ANY),
        out_shape=jax.ShapeDtypeStruct(packed, jnp.bfloat16),
        scratch_shapes=[
            pltpu.VMEM(green_occ.shape, jnp.bfloat16),
            pltpu.VMEM(green_virt.shape, jnp.bfloat16),
            pltpu.VMEM(packed, jnp.bfloat16),
            pltpu.SemaphoreType.DMA((n_block, 2)),
            pltpu.SemaphoreType.DMA((n_block,)),
        ],
        compiler_params=pltpu.CompilerParams(vmem_limit_bytes=60 << 20),
        name="product",
    )(green_occ, green_virt)
    times = lax.all_to_all(product, "tm", split_axis=0, concat_axis=0, tiled=True)

    scale = 1.0 / math.sqrt(NTAU * NG)
    owners = lax.dynamic_slice_in_dim(owner_map, block_offset[0], rows, 0)
    weight = jnp.concatenate([grad_basis.reshape(3 * rows) * scale, jnp.zeros((rows,), jnp.float32)])
    label = jnp.concatenate(
        [jnp.zeros((3 * rows,), jnp.float32), owners.astype(jnp.float32) * (1.0 / (n_col * n_tm))]
    )
    shape = (NTAU, rows, width)
    chi_freq, message = pl.pallas_call(
        transform_kernel,
        out_shape=(
            pltpu.VMEM(shape, jnp.bfloat16),
            jax.ShapeDtypeStruct((CORES * n_near * n_tm, LANES), jnp.float32),
        ),
        compiler_params=pltpu.CompilerParams(vmem_limit_bytes=16 << 20),
        name="transform",
    )(high, low, times, adjoint_w, weight[None, :], label[None, :])

    message = lax.all_to_all(message, ("core", "near", "tm"), split_axis=0, concat_axis=0, tiled=True)
    message = jnp.sum(message.reshape(CORES, n_near * n_tm, LANES), axis=1)
    message = jnp.broadcast_to(message[None], (n_pair * FAR, CORES, LANES))
    message = lax.all_to_all(message, ("pair", "far"), split_axis=0, concat_axis=0, tiled=True)
    forces, chi_freq = pl.pallas_call(
        functools.partial(forces_kernel, rows, FAR),
        out_specs=[pl.BlockSpec(memory_space=pl.ANY)] * 2,
        out_shape=(
            jax.ShapeDtypeStruct((3, NATOM), jnp.float32),
            jax.ShapeDtypeStruct(shape, jnp.bfloat16),
        ),
        scratch_shapes=[pltpu.VMEM((3, NATOM), jnp.float32), pltpu.SemaphoreType.DMA((2,))],
        compiler_params=pltpu.CompilerParams(vmem_limit_bytes=8 << 20),
        name="forces",
    )(message, chi_freq)
    return (chi_freq, forces)


def solution(mesh):
    n_row, n_col, n_tm = (mesh.shape[name] for name in ("row", "col", "tm"))
    n_pair = n_row // CORES
    n_near = n_col // FAR
    axes = ("pair", "core", "near", "far", "tm")
    fine = Mesh(mesh.devices.reshape(n_pair, CORES, n_near, FAR, n_tm), axes)
    row, col = ("pair", "core"), ("near", "far")
    in_specs = (
        P("tm", row, col),
        P("tm", row, col),
        P(None, row, col + ("tm",)),
        P(None, row),
        P(),
        P(row),
    )
    out_specs = (P(None, row, col + ("tm",)), P())
    return jax.shard_map(
        functools.partial(on_device, (n_pair, n_near, n_tm)),
        mesh=fine,
        in_specs=in_specs,
        out_specs=out_specs,
        check_vma=False,
    )
```

```python
import functools
import math

import jax
import jax.numpy as jnp
import ml_dtypes
import numpy as np
from jax import lax
from jax.experimental import pallas as pl
from jax.experimental.pallas import tpu as pltpu
from jax.sharding import Mesh, PartitionSpec as P

NG = 30720
NTAU = 16
NATOM = 1000
GROUP = 16
LANES = 128
SHIFT = 32
QUARTERS = LANES // SHIFT
FULL = 3
CORES = 2
FAR = 2


def transform_matrix():
    steps = np.arange(NTAU, dtype=np.float64)
    table = np.cos(0.1 * 0.15 * 1.35 ** (steps[:, None] + steps[None, :])) / 4.0
    high = table.astype(ml_dtypes.bfloat16)
    low = (table - high.astype(np.float64)).astype(ml_dtypes.bfloat16)
    eye = np.eye(GROUP)
    return [np.kron(part.astype(np.float64), eye).astype(ml_dtypes.bfloat16) for part in (high, low)]


def roll(values, shift):
    return pltpu.roll(values.astype(jnp.float32), shift, 1).astype(values.dtype)


def product_kernel(occ_ref, virt_ref, out_ref, occ, virt, out, in_sems, out_sems):
    n_dest = out_ref.shape[0]
    n_time, rows, _ = occ.shape
    blocks = [(t, pl.ds(start, GROUP)) for t in range(n_time) for start in range(0, rows, GROUP)]
    loads, stores = [], []
    for q, (t, block) in enumerate(blocks):
        pair = [
            pltpu.make_async_copy(src.at[t, block], dst.at[t, block], in_sems.at[q, s])
            for s, (src, dst) in enumerate(((occ_ref, occ), (virt_ref, virt)))
        ]
        for load in pair:
            load.start()
        loads.append(pair)

    def send(part, first, count):
        rows = pl.ds(first * GROUP, count * GROUP)
        store = pltpu.make_async_copy(out.at[:, rows], out_ref.at[:, rows], out_sems.at[part])
        store.start()
        stores.append(store)

    quarter = lax.broadcasted_iota(jnp.int32, (GROUP, LANES), 1) // SHIFT
    rests = {}
    for q, (t, block) in enumerate(blocks):
        for load in loads[q]:
            load.wait()

        def tile(k):
            columns = pl.ds(k * LANES, LANES)
            return occ[t, block, columns] * virt[t, block, columns]

        for j in range(n_dest):
            start = j * (FULL * QUARTERS + QUARTERS - 1)
            head = -start % QUARTERS
            hole = QUARTERS - 1 - head
            first = (start + head) // QUARTERS
            for m in range(FULL):
                out[j, pl.ds((q * FULL + m) * GROUP, GROUP), :] = tile(first + m)
            if head == 0:
                rest = tile(first + FULL)
            elif hole == 0:
                rest = tile(first - 1)
            else:
                rest = jnp.where(quarter > hole, tile(first - 1), tile(first + FULL))
            rests[j, q] = rest
        if q < len(blocks) - 1:
            send(q, q * FULL, FULL)
            continue
        for j in range(n_dest):
            hole = QUARTERS - 1 - -j * (FULL * QUARTERS + QUARTERS - 1) % QUARTERS
            for m in range(FULL):
                moved = roll(rests[j, q], LANES - (1 + m) * SHIFT)
                filled = jnp.where(quarter == hole, moved, rests[j, m])
                out[j, pl.ds(((q + 1) * FULL + m) * GROUP, GROUP), :] = filled
        send(q, q * FULL, 2 * FULL)
    for store in stores:
        store.wait()


def own_place():
    head = lax.rem(lax.axis_index("tm"), QUARTERS)
    return head, QUARTERS - 1 - head


def transformed(high_ref, low_ref, values):
    total = jnp.dot(high_ref[...], values, preferred_element_type=jnp.float32)
    return total + jnp.dot(low_ref[...], values, preferred_element_type=jnp.float32)


def adjoint_kernel(high_ref, low_ref, adjoint_ref, out_ref):
    n_freq, rows, width = adjoint_ref.shape
    n_source = out_ref.shape[0]
    per_source, halves = n_freq // n_source, rows // GROUP
    n_block = per_source * halves
    head, hole = own_place()
    split = LANES - head * SHIFT
    quarter = lax.broadcasted_iota(jnp.int32, (GROUP, LANES), 1) // SHIFT
    wide = lax.broadcasted_iota(jnp.int32, (n_freq * GROUP, LANES), 1)
    rests = {}
    for half in range(halves):
        block = pl.ds(half * GROUP, GROUP)
        values = adjoint_ref[:, block, :].reshape(n_freq * GROUP, width)
        total = transformed(high_ref, low_ref, values)
        pad = jnp.zeros((n_freq * GROUP, (FULL + 1) * LANES - width), jnp.float32)
        total = jnp.concatenate([total, pad], axis=1)
        turned = [
            pltpu.roll(total[:, m * LANES : (m + 1) * LANES], lax.rem(split, LANES), 1)
            for m in range(FULL + 1)
        ]
        packed = [jnp.where(wide < split, turned[m], turned[m + 1]) for m in range(FULL)]
        rest = jnp.where(wide < split, turned[FULL], turned[0])
        for t in range(n_freq):
            i, tt = divmod(t, per_source)
            q = tt * halves + half
            lines = slice(t * GROUP, (t + 1) * GROUP)
            for m in range(FULL):
                out_ref[i, pl.ds((q * FULL + m) * GROUP, GROUP), :] = packed[m][lines]
            rests[i, q] = rest[lines]
    for i in range(n_source):
        for m in range(FULL):
            moved = pltpu.roll(rests[i, n_block - 1], LANES - (1 + m) * SHIFT, 1)
            filled = jnp.where(quarter == hole, moved, rests[i, m])
            out_ref[i, pl.ds((n_block * FULL + m) * GROUP, GROUP), :] = filled


def energy_kernel(rows, times_ref, adjoint_ref, weight_ref, label_ref, message_ref):
    n_source, lines, _ = times_ref.shape
    n_block = lines // GROUP // FULL - 1
    halves = rows // GROUP
    _, hole = own_place()
    in_hole = lax.broadcasted_iota(jnp.int32, (GROUP, LANES), 1) // SHIFT == hole
    sums = [jnp.zeros((GROUP, LANES), jnp.float32) for _ in range(halves)]

    def terms(tile):
        lines = pl.ds(tile * GROUP, GROUP)
        total = jnp.zeros((GROUP, LANES), jnp.float32)
        for i in range(n_source):
            total += times_ref[i, lines, :].astype(jnp.float32) * adjoint_ref[i, lines, :]
        return total

    for q in range(n_block):
        for m in range(FULL):
            sums[q % halves] += terms(q * FULL + m)
    for m in range(FULL):
        rest = terms(n_block * FULL + m)
        sums[m % halves] += jnp.where(in_hole, 0.0, rest)
        sums[(n_block - 1) % halves] += jnp.where(in_hole, rest, 0.0)
    total = jnp.zeros((1, LANES), jnp.float32)
    for half in range(halves):
        energy = jnp.sum(sums[half], axis=1, keepdims=True)
        row = lax.broadcasted_iota(jnp.int32, (GROUP, LANES), 0) + half * GROUP
        lane = lax.broadcasted_iota(jnp.int32, (GROUP, LANES), 1)
        total += jnp.sum(jnp.where(lane % rows == row, energy, 0.0), axis=0, keepdims=True)
    message = total * weight_ref[...] + label_ref[...]
    message_ref[...] = jnp.broadcast_to(message, message_ref.shape)


def write_chi(high_ref, low_ref, times_ref, chi_ref, done):
    n_source = times_ref.shape[0]
    n_freq, rows, width = chi_ref.shape
    head, hole = own_place()
    turn = head * SHIFT
    quarter = lax.broadcasted_iota(jnp.int32, (GROUP, LANES), 1) // SHIFT
    wide = lax.broadcasted_iota(jnp.int32, (n_freq * GROUP, LANES), 1)
    n_block = NTAU // n_source * (rows // GROUP)

    def stored(i, tile):
        return times_ref[i, pl.ds(tile * GROUP, GROUP), :]

    def last_rest(i):
        rest = stored(i, n_block * FULL)
        for m in range(FULL):
            moved = roll(stored(i, n_block * FULL + m), (1 + m) * SHIFT)
            rest = jnp.where(quarter == lax.rem(hole + 1 + m, QUARTERS), moved, rest)
        return rest

    def column_tile(half, m):
        parts = []
        for t in range(NTAU):
            i, tt = divmod(t, NTAU // n_source)
            q = tt * (rows // GROUP) + half
            if m < FULL:
                parts.append(stored(i, q * FULL + m))
            elif q < n_block - 1:
                parts.append(stored(i, n_block * FULL + q))
            else:
                parts.append(last_rest(i))
        return jnp.concatenate(parts, axis=0)

    for half in range(rows // GROUP):
        block = pl.ds(half * GROUP, GROUP)
        values = jnp.concatenate([column_tile(half, m) for m in range(FULL + 1)], axis=1)
        chi = transformed(high_ref, low_ref, values)
        turned = [pltpu.roll(chi[:, m * LANES : (m + 1) * LANES], turn, 1) for m in range(FULL + 1)]
        for m in range(FULL + 1):
            count = min(LANES, width - m * LANES)
            natural = jnp.where(wide < turn, turned[m - 1], turned[m])[:, :count]
            natural = natural.astype(jnp.bfloat16).reshape(n_freq, GROUP, count)
            chi_ref[:, block, pl.ds(m * LANES, count)] = natural
        done(half, block)


def forces_kernel(
    rows, n_col, message_ref, high_ref, low_ref, times_ref,
    forces_out_ref, chi_out_ref, forces_ref, chi_ref, sems,
):
    stores = []

    def send(half, block):
        store = pltpu.make_async_copy(chi_ref.at[:, block], chi_out_ref.at[:, block], sems.at[half])
        store.start()
        stores.append(store)

    write_chi(high_ref, low_ref, times_ref, chi_ref, send)
    sums = []
    for block in range(message_ref.shape[0] // n_col * CORES):
        pair, core = divmod(block, CORES)
        devices = pl.ds(pair * n_col, n_col)
        sums.append(jnp.sum(message_ref[devices, core, :], axis=0, keepdims=True))
    parts = [
        jnp.concatenate([total[:, p * rows : (p + 1) * rows] for total in sums], axis=1)
        for p in range(4)
    ]
    owners = parts[3].astype(jnp.int32)
    weights = jnp.concatenate(parts[:3] + [jnp.zeros_like(parts[0])] * 5, axis=0)
    upper, lower = owners // LANES, owners % LANES
    n_upper = pl.cdiv(NATOM, LANES)
    rest = jnp.concatenate([jnp.where(upper == u, weights, 0.0) for u in range(n_upper)], axis=0)
    lanes = lax.broadcasted_iota(jnp.int32, (LANES, owners.shape[1]), 0)
    onehot = jnp.where(lanes == lower, 1.0, 0.0).astype(jnp.bfloat16)
    forces = jnp.zeros((8 * n_upper, LANES), jnp.float32)
    for _ in range(3):
        part = rest.astype(jnp.bfloat16)
        rest = rest - part.astype(jnp.float32)
        forces += lax.dot_general(
            part, onehot, (((1,), (1,)), ((), ())), preferred_element_type=jnp.float32
        )
    for u in range(n_upper):
        count = min(LANES, NATOM - u * LANES)
        forces_ref[:, u * LANES : u * LANES + count] = forces[u * 8 : u * 8 + 3, :count]
    store = pltpu.make_async_copy(forces_ref, forces_out_ref, sems.at[rows // GROUP])
    store.start()
    for store in [*stores, store]:
        store.wait()


def on_device(sizes, green_occ, green_virt, adjoint_w, grad_basis, owner_map, block_offset):
    n_pair, n_near, n_tm = sizes
    n_col = n_near * FAR
    n_time, rows, columns = green_occ.shape
    width = columns // n_tm
    high, low = (jnp.asarray(part) for part in transform_matrix())
    n_block = n_time * rows // GROUP
    tiles = n_block * FULL + FULL
    assert width == FULL * LANES + (QUARTERS - 1) * SHIFT and n_block == FULL + 1

    packed = (n_tm, tiles * GROUP, LANES)
    product = pl.pallas_call(
        product_kernel,
        in_specs=[pl.BlockSpec(memory_space=pl.ANY)] * 2,
        out_specs=pl.BlockSpec(memory_space=pl.ANY),
        out_shape=jax.ShapeDtypeStruct(packed, jnp.bfloat16),
        scratch_shapes=[
            pltpu.VMEM(green_occ.shape, jnp.bfloat16),
            pltpu.VMEM(green_virt.shape, jnp.bfloat16),
            pltpu.VMEM(packed, jnp.bfloat16),
            pltpu.SemaphoreType.DMA((n_block, 2)),
            pltpu.SemaphoreType.DMA((n_block,)),
        ],
        compiler_params=pltpu.CompilerParams(vmem_limit_bytes=60 << 20),
        name="product",
    )(green_occ, green_virt)
    times = lax.all_to_all(product, "tm", split_axis=0, concat_axis=0, tiled=True)

    def kernel(body, name, shape, dtype, limit, *operands):
        elements = NTAU * rows * width
        return pl.pallas_call(
            body,
            out_shape=jax.ShapeDtypeStruct(shape, dtype),
            cost_estimate=pl.CostEstimate(
                flops=4 * NTAU * GROUP * elements, bytes_accessed=4 * elements, transcendentals=0
            ),
            compiler_params=pltpu.CompilerParams(vmem_limit_bytes=limit << 20),
            name=name,
        )(*operands)

    scale = 1.0 / math.sqrt(NTAU * NG)
    owners = lax.dynamic_slice_in_dim(owner_map, block_offset[0], rows, 0)
    weight = jnp.concatenate([grad_basis.reshape(3 * rows) * scale, jnp.zeros((rows,), jnp.float32)])
    label = jnp.concatenate(
        [jnp.zeros((3 * rows,), jnp.float32), owners.astype(jnp.float32) * (1.0 / (n_col * n_tm))]
    )
    adjoint = kernel(adjoint_kernel, "adjoint", packed, jnp.float32, 16, high, low, adjoint_w)
    message = pl.pallas_call(
        functools.partial(energy_kernel, rows),
        out_shape=jax.ShapeDtypeStruct((CORES * n_near * n_tm, LANES), jnp.float32),
        compiler_params=pltpu.CompilerParams(vmem_limit_bytes=16 << 20),
        name="energy",
    )(times, adjoint, weight[None, :], label[None, :])

    message = lax.all_to_all(message, ("core", "near", "tm"), split_axis=0, concat_axis=0, tiled=True)
    message = jnp.sum(message.reshape(CORES, n_near * n_tm, LANES), axis=1)
    message = jnp.broadcast_to(message[None], (n_pair * FAR, CORES, LANES))
    message = lax.all_to_all(message, ("pair", "far"), split_axis=0, concat_axis=0, tiled=True)
    shape = (NTAU, rows, width)
    forces, chi_freq = pl.pallas_call(
        functools.partial(forces_kernel, rows, FAR),
        out_specs=[pl.BlockSpec(memory_space=pl.ANY)] * 2,
        out_shape=(
            jax.ShapeDtypeStruct((3, NATOM), jnp.float32),
            jax.ShapeDtypeStruct(shape, jnp.bfloat16),
        ),
        scratch_shapes=[
            pltpu.VMEM((3, NATOM), jnp.float32),
            pltpu.VMEM(shape, jnp.bfloat16),
            pltpu.SemaphoreType.DMA((rows // GROUP + 1,)),
        ],
        compiler_params=pltpu.CompilerParams(vmem_limit_bytes=16 << 20),
        name="forces",
    )(message, high, low, times)
    return (chi_freq, forces)


def solution(mesh):
    n_row, n_col, n_tm = (mesh.shape[name] for name in ("row", "col", "tm"))
    n_pair = n_row // CORES
    n_near = n_col // FAR
    axes = ("pair", "core", "near", "far", "tm")
    fine = Mesh(mesh.devices.reshape(n_pair, CORES, n_near, FAR, n_tm), axes)
    row, col = ("pair", "core"), ("near", "far")
    in_specs = (
        P("tm", row, col),
        P("tm", row, col),
        P(None, row, col + ("tm",)),
        P(None, row),
        P(),
        P(row),
    )
    out_specs = (P(None, row, col + ("tm",)), P())
    return jax.shard_map(
        functools.partial(on_device, (n_pair, n_near, n_tm)),
        mesh=fine,
        in_specs=in_specs,
        out_specs=out_specs,
        check_vma=False,
    )
```

```python
import functools
import math

import jax
import jax.numpy as jnp
import ml_dtypes
import numpy as np
from jax import lax
from jax.experimental import pallas as pl
from jax.experimental.pallas import tpu as pltpu
from jax.sharding import Mesh, PartitionSpec as P

NG = 30720
NTAU = 16
NATOM = 1000
GROUP = 16
LANES = 128
SHIFT = 32
QUARTERS = LANES // SHIFT
FULL = 3
CORES = 2
FAR = 2


def transform_matrix():
    steps = np.arange(NTAU, dtype=np.float64)
    table = np.cos(0.1 * 0.15 * 1.35 ** (steps[:, None] + steps[None, :])) / 4.0
    high = table.astype(ml_dtypes.bfloat16)
    low = (table - high.astype(np.float64)).astype(ml_dtypes.bfloat16)
    eye = np.eye(GROUP)
    return [np.kron(part.astype(np.float64), eye).astype(ml_dtypes.bfloat16) for part in (high, low)]


def roll(values, shift):
    return pltpu.roll(values.astype(jnp.float32), shift, 1).astype(values.dtype)


def product_kernel(occ_ref, virt_ref, out_ref, occ, virt, out, in_sems, out_sems):
    n_dest = out_ref.shape[0]
    n_time, rows, _ = occ.shape
    blocks = [(t, pl.ds(start, GROUP)) for t in range(n_time) for start in range(0, rows, GROUP)]
    loads, stores = [], []
    for q, (t, block) in enumerate(blocks):
        pair = [
            pltpu.make_async_copy(src.at[t, block], dst.at[t, block], in_sems.at[q, s])
            for s, (src, dst) in enumerate(((occ_ref, occ), (virt_ref, virt)))
        ]
        for load in pair:
            load.start()
        loads.append(pair)

    def send(part, first, count):
        rows = pl.ds(first * GROUP, count * GROUP)
        store = pltpu.make_async_copy(out.at[:, rows], out_ref.at[:, rows], out_sems.at[part])
        store.start()
        stores.append(store)

    quarter = lax.broadcasted_iota(jnp.int32, (GROUP, LANES), 1) // SHIFT
    rests = {}
    for q, (t, block) in enumerate(blocks):
        for load in loads[q]:
            load.wait()

        def tile(k):
            columns = pl.ds(k * LANES, LANES)
            return occ[t, block, columns] * virt[t, block, columns]

        for j in range(n_dest):
            start = j * (FULL * QUARTERS + QUARTERS - 1)
            head = -start % QUARTERS
            hole = QUARTERS - 1 - head
            first = (start + head) // QUARTERS
            for m in range(FULL):
                out[j, pl.ds((q * FULL + m) * GROUP, GROUP), :] = tile(first + m)
            if head == 0:
                rest = tile(first + FULL)
            elif hole == 0:
                rest = tile(first - 1)
            else:
                rest = jnp.where(quarter > hole, tile(first - 1), tile(first + FULL))
            rests[j, q] = rest
        if q < len(blocks) - 1:
            send(q, q * FULL, FULL)
            continue
        for j in range(n_dest):
            hole = QUARTERS - 1 - -j * (FULL * QUARTERS + QUARTERS - 1) % QUARTERS
            for m in range(FULL):
                moved = roll(rests[j, q], LANES - (1 + m) * SHIFT)
                filled = jnp.where(quarter == hole, moved, rests[j, m])
                out[j, pl.ds(((q + 1) * FULL + m) * GROUP, GROUP), :] = filled
        send(q, q * FULL, 2 * FULL)
    for store in stores:
        store.wait()


def own_place():
    head = lax.rem(lax.axis_index("tm"), QUARTERS)
    return head, QUARTERS - 1 - head


def transformed(high_ref, low_ref, values):
    total = jnp.dot(high_ref[...], values, preferred_element_type=jnp.float32)
    return total + jnp.dot(low_ref[...], values, preferred_element_type=jnp.float32)


def adjoint_kernel(high_ref, low_ref, adjoint_ref, out_ref):
    n_freq, rows, width = adjoint_ref.shape
    n_source = out_ref.shape[0]
    per_source, halves = n_freq // n_source, rows // GROUP
    n_block = per_source * halves
    head, hole = own_place()
    split = LANES - head * SHIFT
    quarter = lax.broadcasted_iota(jnp.int32, (GROUP, LANES), 1) // SHIFT
    wide = lax.broadcasted_iota(jnp.int32, (n_freq * GROUP, LANES), 1)
    rests = {}
    for half in range(halves):
        block = pl.ds(half * GROUP, GROUP)
        values = adjoint_ref[:, block, :].reshape(n_freq * GROUP, width)
        total = transformed(high_ref, low_ref, values)
        pad = jnp.zeros((n_freq * GROUP, (FULL + 1) * LANES - width), jnp.float32)
        total = jnp.concatenate([total, pad], axis=1)
        turned = [
            pltpu.roll(total[:, m * LANES : (m + 1) * LANES], lax.rem(split, LANES), 1)
            for m in range(FULL + 1)
        ]
        packed = [jnp.where(wide < split, turned[m], turned[m + 1]) for m in range(FULL)]
        rest = jnp.where(wide < split, turned[FULL], turned[0])
        for t in range(n_freq):
            i, tt = divmod(t, per_source)
            q = tt * halves + half
            lines = slice(t * GROUP, (t + 1) * GROUP)
            for m in range(FULL):
                out_ref[i, pl.ds((q * FULL + m) * GROUP, GROUP), :] = packed[m][lines]
            rests[i, q] = rest[lines]
    for i in range(n_source):
        for m in range(FULL):
            moved = pltpu.roll(rests[i, n_block - 1], LANES - (1 + m) * SHIFT, 1)
            filled = jnp.where(quarter == hole, moved, rests[i, m])
            out_ref[i, pl.ds((n_block * FULL + m) * GROUP, GROUP), :] = filled


def energy_kernel(rows, times_ref, adjoint_ref, weight_ref, label_ref, message_ref):
    n_source, lines, _ = times_ref.shape
    n_block = lines // GROUP // FULL - 1
    halves = rows // GROUP
    _, hole = own_place()
    in_hole = lax.broadcasted_iota(jnp.int32, (GROUP, LANES), 1) // SHIFT == hole
    sums = [jnp.zeros((GROUP, LANES), jnp.float32) for _ in range(halves)]

    def terms(tile):
        lines = pl.ds(tile * GROUP, GROUP)
        total = jnp.zeros((GROUP, LANES), jnp.float32)
        for i in range(n_source):
            total += times_ref[i, lines, :].astype(jnp.float32) * adjoint_ref[i, lines, :]
        return total

    for q in range(n_block):
        for m in range(FULL):
            sums[q % halves] += terms(q * FULL + m)
    for m in range(FULL):
        rest = terms(n_block * FULL + m)
        sums[m % halves] += jnp.where(in_hole, 0.0, rest)
        sums[(n_block - 1) % halves] += jnp.where(in_hole, rest, 0.0)
    total = jnp.zeros((1, LANES), jnp.float32)
    for half in range(halves):
        energy = jnp.sum(sums[half], axis=1, keepdims=True)
        row = lax.broadcasted_iota(jnp.int32, (GROUP, LANES), 0) + half * GROUP
        lane = lax.broadcasted_iota(jnp.int32, (GROUP, LANES), 1)
        total += jnp.sum(jnp.where(lane % rows == row, energy, 0.0), axis=0, keepdims=True)
    message = total * weight_ref[...] + label_ref[...]
    message_ref[...] = jnp.broadcast_to(message, message_ref.shape)


def write_chi(high_ref, low_ref, times_ref, chi_ref, done):
    n_source = times_ref.shape[0]
    n_freq, rows, width = chi_ref.shape
    head, hole = own_place()
    turn = head * SHIFT
    quarter = lax.broadcasted_iota(jnp.int32, (GROUP, LANES), 1) // SHIFT
    wide = lax.broadcasted_iota(jnp.int32, (n_freq * GROUP, LANES), 1)
    n_block = NTAU // n_source * (rows // GROUP)

    def stored(i, tile):
        return times_ref[i, pl.ds(tile * GROUP, GROUP), :]

    def last_rest(i):
        rest = stored(i, n_block * FULL)
        for m in range(FULL):
            moved = roll(stored(i, n_block * FULL + m), (1 + m) * SHIFT)
            rest = jnp.where(quarter == lax.rem(hole + 1 + m, QUARTERS), moved, rest)
        return rest

    def column_tile(half, m):
        parts = []
        for t in range(NTAU):
            i, tt = divmod(t, NTAU // n_source)
            q = tt * (rows // GROUP) + half
            if m < FULL:
                parts.append(stored(i, q * FULL + m))
            elif q < n_block - 1:
                parts.append(stored(i, n_block * FULL + q))
            else:
                parts.append(last_rest(i))
        return jnp.concatenate(parts, axis=0)

    for half in range(rows // GROUP):
        block = pl.ds(half * GROUP, GROUP)
        values = jnp.concatenate([column_tile(half, m) for m in range(FULL + 1)], axis=1)
        chi = transformed(high_ref, low_ref, values)
        turned = [pltpu.roll(chi[:, m * LANES : (m + 1) * LANES], turn, 1) for m in range(FULL + 1)]
        for m in range(FULL + 1):
            count = min(LANES, width - m * LANES)
            natural = jnp.where(wide < turn, turned[m - 1], turned[m])[:, :count]
            natural = natural.astype(jnp.bfloat16).reshape(n_freq, GROUP, count)
            chi_ref[:, block, pl.ds(m * LANES, count)] = natural
        done(half, block)


def forces_kernel(
    rows, n_col, message_ref, high_ref, low_ref, times_ref,
    forces_out_ref, chi_out_ref, forces_ref, chi_ref, sems,
):
    stores = []

    def send(half, block):
        store = pltpu.make_async_copy(chi_ref.at[:, block], chi_out_ref.at[:, block], sems.at[half])
        store.start()
        stores.append(store)

    write_chi(high_ref, low_ref, times_ref, chi_ref, send)
    n_pair = message_ref.shape[0] // n_col
    sums = []
    for pair in range(n_pair):
        total = message_ref[pair * n_col]
        for i in range(1, n_col):
            total += message_ref[pair * n_col + i]
        sums.append(total)
    sums = jnp.concatenate(sums, axis=0)
    n_block = n_pair * CORES
    block = lax.broadcasted_iota(jnp.int32, (n_block, LANES), 0)
    quarter = lax.broadcasted_iota(jnp.int32, (n_block, LANES), 1) // rows
    own = quarter == block % QUARTERS
    turned = [sums if d == 0 else pltpu.roll(sums, d * rows, 1) for d in range(QUARTERS)]

    def along_lanes(part):
        placed = jnp.zeros((n_block, LANES), jnp.float32)
        for d in range(QUARTERS):
            placed = jnp.where(own & (quarter == (part + d) % QUARTERS), turned[d], placed)
        tiles = [
            jnp.sum(jnp.where(block // QUARTERS == tile, placed, 0.0), axis=0, keepdims=True)
            for tile in range(n_block // QUARTERS)
        ]
        return jnp.concatenate(tiles, axis=1)

    owners = along_lanes(3).astype(jnp.int32)
    width = n_block * rows
    part = lax.broadcasted_iota(jnp.int32, (8, width), 0)
    weights = jnp.zeros((8, width), jnp.float32)
    for p in range(3):
        weights = jnp.where(part == p, along_lanes(p), weights)
    upper, lower = owners // LANES, owners % LANES
    n_upper = pl.cdiv(NATOM, LANES)
    lanes = lax.broadcasted_iota(jnp.int32, (LANES, width), 0)
    onehot = jnp.where(lanes == lower, 1.0, 0.0).astype(jnp.bfloat16)
    pieces = []
    rest = weights
    for _ in range(3):
        piece = rest.astype(jnp.bfloat16).astype(jnp.float32)
        rest = rest - piece
        pieces += [jnp.where(upper == u, piece, 0.0) for u in range(n_upper)]
    pieces = jnp.concatenate(pieces, axis=0).astype(jnp.bfloat16)
    products = lax.dot_general(
        pieces, onehot, (((1,), (1,)), ((), ())), preferred_element_type=jnp.float32
    )
    count = 8 * n_upper
    forces = products[:count] + products[count : 2 * count] + products[2 * count :]
    for u in range(n_upper):
        count = min(LANES, NATOM - u * LANES)
        forces_ref[:, u * LANES : u * LANES + count] = forces[u * 8 : u * 8 + 3, :count]
    store = pltpu.make_async_copy(forces_ref, forces_out_ref, sems.at[rows // GROUP])
    store.start()
    for store in [*stores, store]:
        store.wait()


def on_device(sizes, green_occ, green_virt, adjoint_w, grad_basis, owner_map, block_offset):
    n_pair, n_near, n_tm = sizes
    n_col = n_near * FAR
    n_time, rows, columns = green_occ.shape
    width = columns // n_tm
    high, low = (jnp.asarray(part) for part in transform_matrix())
    n_block = n_time * rows // GROUP
    tiles = n_block * FULL + FULL
    assert width == FULL * LANES + (QUARTERS - 1) * SHIFT and n_block == FULL + 1

    packed = (n_tm, tiles * GROUP, LANES)
    product = pl.pallas_call(
        product_kernel,
        in_specs=[pl.BlockSpec(memory_space=pl.ANY)] * 2,
        out_specs=pl.BlockSpec(memory_space=pl.ANY),
        out_shape=jax.ShapeDtypeStruct(packed, jnp.bfloat16),
        scratch_shapes=[
            pltpu.VMEM(green_occ.shape, jnp.bfloat16),
            pltpu.VMEM(green_virt.shape, jnp.bfloat16),
            pltpu.VMEM(packed, jnp.bfloat16),
            pltpu.SemaphoreType.DMA((n_block, 2)),
            pltpu.SemaphoreType.DMA((n_block,)),
        ],
        compiler_params=pltpu.CompilerParams(vmem_limit_bytes=60 << 20),
        name="product",
    )(green_occ, green_virt)
    times = lax.all_to_all(product, "tm", split_axis=0, concat_axis=0, tiled=True)

    def kernel(body, name, shape, dtype, limit, *operands):
        elements = NTAU * rows * width
        return pl.pallas_call(
            body,
            out_shape=jax.ShapeDtypeStruct(shape, dtype),
            cost_estimate=pl.CostEstimate(
                flops=4 * NTAU * GROUP * elements, bytes_accessed=4 * elements, transcendentals=0
            ),
            compiler_params=pltpu.CompilerParams(vmem_limit_bytes=limit << 20),
            name=name,
        )(*operands)

    scale = 1.0 / math.sqrt(NTAU * NG)
    owners = lax.dynamic_slice_in_dim(owner_map, block_offset[0], rows, 0)
    weight = jnp.concatenate([grad_basis.reshape(3 * rows) * scale, jnp.zeros((rows,), jnp.float32)])
    label = jnp.concatenate(
        [jnp.zeros((3 * rows,), jnp.float32), owners.astype(jnp.float32) * (1.0 / (n_col * n_tm))]
    )
    adjoint = kernel(adjoint_kernel, "adjoint", packed, jnp.float32, 16, high, low, adjoint_w)
    message = pl.pallas_call(
        functools.partial(energy_kernel, rows),
        out_shape=jax.ShapeDtypeStruct((CORES * n_near * n_tm, LANES), jnp.float32),
        compiler_params=pltpu.CompilerParams(vmem_limit_bytes=16 << 20),
        name="energy",
    )(times, adjoint, weight[None, :], label[None, :])

    message = lax.all_to_all(message, ("core", "near", "tm"), split_axis=0, concat_axis=0, tiled=True)
    message = jnp.sum(message.reshape(CORES, n_near * n_tm, LANES), axis=1)
    message = jnp.broadcast_to(message[None], (n_pair * FAR, CORES, LANES))
    message = lax.all_to_all(message, ("pair", "far"), split_axis=0, concat_axis=0, tiled=True)
    shape = (NTAU, rows, width)
    forces, chi_freq = pl.pallas_call(
        functools.partial(forces_kernel, rows, FAR),
        out_specs=[pl.BlockSpec(memory_space=pl.ANY)] * 2,
        out_shape=(
            jax.ShapeDtypeStruct((3, NATOM), jnp.float32),
            jax.ShapeDtypeStruct(shape, jnp.bfloat16),
        ),
        scratch_shapes=[
            pltpu.VMEM((3, NATOM), jnp.float32),
            pltpu.VMEM(shape, jnp.bfloat16),
            pltpu.SemaphoreType.DMA((rows // GROUP + 1,)),
        ],
        compiler_params=pltpu.CompilerParams(vmem_limit_bytes=16 << 20),
        name="forces",
    )(message, high, low, times)
    return (chi_freq, forces)


def solution(mesh):
    n_row, n_col, n_tm = (mesh.shape[name] for name in ("row", "col", "tm"))
    n_pair = n_row // CORES
    n_near = n_col // FAR
    axes = ("pair", "core", "near", "far", "tm")
    fine = Mesh(mesh.devices.reshape(n_pair, CORES, n_near, FAR, n_tm), axes)
    row, col = ("pair", "core"), ("near", "far")
    in_specs = (
        P("tm", row, col),
        P("tm", row, col),
        P(None, row, col + ("tm",)),
        P(None, row),
        P(),
        P(row),
    )
    out_specs = (P(None, row, col + ("tm",)), P())
    return jax.shard_map(
        functools.partial(on_device, (n_pair, n_near, n_tm)),
        mesh=fine,
        in_specs=in_specs,
        out_specs=out_specs,
        check_vma=False,
    )
```

```python
import functools
import math

import jax
import jax.numpy as jnp
import ml_dtypes
import numpy as np
from jax import lax
from jax.experimental import pallas as pl
from jax.experimental.pallas import tpu as pltpu
from jax.sharding import Mesh, PartitionSpec as P

NG = 30720
NTAU = 16
NATOM = 1000
GROUP = 16
LANES = 128
SHIFT = 32
QUARTERS = LANES // SHIFT
FULL = 3
ORDER = (0, 2, 4, 6, 1, 3, 5, 7)
CORES = 2
FAR = 2


def transform_matrix():
    steps = np.arange(NTAU, dtype=np.float64)
    table = np.cos(0.1 * 0.15 * 1.35 ** (steps[:, None] + steps[None, :])) / 4.0
    high = table.astype(ml_dtypes.bfloat16)
    low = (table - high.astype(np.float64)).astype(ml_dtypes.bfloat16)
    eye = np.eye(GROUP)
    return [np.kron(part.astype(np.float64), eye).astype(ml_dtypes.bfloat16) for part in (high, low)]


def roll(values, shift):
    return pltpu.roll(values.astype(jnp.float32), shift, 1).astype(values.dtype)


def product_kernel(occ_ref, virt_ref, out_ref, occ, virt, out, in_sems, out_sems):
    n_dest = out_ref.shape[0]
    n_time, rows, _ = occ.shape
    blocks = [(t, pl.ds(start, GROUP)) for t in range(n_time) for start in range(0, rows, GROUP)]
    loads, stores = [], []
    for q, (t, block) in enumerate(blocks):
        pair = [
            pltpu.make_async_copy(src.at[t, block], dst.at[t, block], in_sems.at[q, s])
            for s, (src, dst) in enumerate(((occ_ref, occ), (virt_ref, virt)))
        ]
        for load in pair:
            load.start()
        loads.append(pair)

    def send(part, first, count):
        rows = pl.ds(first * GROUP, count * GROUP)
        store = pltpu.make_async_copy(out.at[:, rows], out_ref.at[:, rows], out_sems.at[part])
        store.start()
        stores.append(store)

    quarter = lax.broadcasted_iota(jnp.int32, (GROUP, LANES), 1) // SHIFT
    rests = {}
    for q, (t, block) in enumerate(blocks):
        for load in loads[q]:
            load.wait()

        def tile(k):
            columns = pl.ds(k * LANES, LANES)
            return occ[t, block, columns] * virt[t, block, columns]

        for j in range(n_dest):
            start = j * (FULL * QUARTERS + QUARTERS - 1)
            head = -start % QUARTERS
            hole = QUARTERS - 1 - head
            first = (start + head) // QUARTERS
            for m in range(FULL):
                out[ORDER.index(j), pl.ds((q * FULL + m) * GROUP, GROUP), :] = tile(first + m)
            if head == 0:
                rest = tile(first + FULL)
            elif hole == 0:
                rest = tile(first - 1)
            else:
                rest = jnp.where(quarter > hole, tile(first - 1), tile(first + FULL))
            rests[j, q] = rest
        if q < len(blocks) - 1:
            send(q, q * FULL, FULL)
            continue
        for j in range(n_dest):
            hole = QUARTERS - 1 - -j * (FULL * QUARTERS + QUARTERS - 1) % QUARTERS
            for m in range(FULL):
                moved = roll(rests[j, q], LANES - (1 + m) * SHIFT)
                filled = jnp.where(quarter == hole, moved, rests[j, m])
                out[ORDER.index(j), pl.ds(((q + 1) * FULL + m) * GROUP, GROUP), :] = filled
        send(q, q * FULL, 2 * FULL)
    for store in stores:
        store.wait()


def own_place():
    head = lax.rem(lax.axis_index("tm"), QUARTERS)
    return head, QUARTERS - 1 - head


def transformed(high_ref, low_ref, values):
    total = jnp.dot(high_ref[...], values, preferred_element_type=jnp.float32)
    return total + jnp.dot(low_ref[...], values, preferred_element_type=jnp.float32)


def adjoint_kernel(high_ref, low_ref, adjoint_ref, out_ref):
    n_freq, rows, width = adjoint_ref.shape
    n_source = out_ref.shape[0]
    per_source, halves = n_freq // n_source, rows // GROUP
    n_block = per_source * halves
    head, hole = own_place()
    split = LANES - head * SHIFT
    quarter = lax.broadcasted_iota(jnp.int32, (GROUP, LANES), 1) // SHIFT
    wide = lax.broadcasted_iota(jnp.int32, (n_freq * GROUP, LANES), 1)
    rests = {}
    for half in range(halves):
        block = pl.ds(half * GROUP, GROUP)
        values = adjoint_ref[:, block, :].reshape(n_freq * GROUP, width)
        total = transformed(high_ref, low_ref, values)
        pad = jnp.zeros((n_freq * GROUP, (FULL + 1) * LANES - width), jnp.float32)
        total = jnp.concatenate([total, pad], axis=1)
        turned = [
            pltpu.roll(total[:, m * LANES : (m + 1) * LANES], lax.rem(split, LANES), 1)
            for m in range(FULL + 1)
        ]
        packed = [jnp.where(wide < split, turned[m], turned[m + 1]) for m in range(FULL)]
        rest = jnp.where(wide < split, turned[FULL], turned[0])
        for t in range(n_freq):
            i, tt = divmod(t, per_source)
            q = tt * halves + half
            lines = slice(t * GROUP, (t + 1) * GROUP)
            for m in range(FULL):
                out_ref[ORDER.index(i), pl.ds((q * FULL + m) * GROUP, GROUP), :] = packed[m][lines]
            rests[i, q] = rest[lines]
    for i in range(n_source):
        for m in range(FULL):
            moved = pltpu.roll(rests[i, n_block - 1], LANES - (1 + m) * SHIFT, 1)
            filled = jnp.where(quarter == hole, moved, rests[i, m])
            out_ref[ORDER.index(i), pl.ds((n_block * FULL + m) * GROUP, GROUP), :] = filled


def energy_kernel(rows, times_ref, adjoint_ref, weight_ref, label_ref, message_ref):
    n_source, lines, _ = times_ref.shape
    n_block = lines // GROUP // FULL - 1
    halves = rows // GROUP
    _, hole = own_place()
    in_hole = lax.broadcasted_iota(jnp.int32, (GROUP, LANES), 1) // SHIFT == hole
    sums = [jnp.zeros((GROUP, LANES), jnp.float32) for _ in range(halves)]

    def terms(tile):
        lines = pl.ds(tile * GROUP, GROUP)
        total = jnp.zeros((GROUP, LANES), jnp.float32)
        for i in range(n_source):
            total += times_ref[i, lines, :].astype(jnp.float32) * adjoint_ref[i, lines, :]
        return total

    for q in range(n_block):
        for m in range(FULL):
            sums[q % halves] += terms(q * FULL + m)
    for m in range(FULL):
        rest = terms(n_block * FULL + m)
        sums[m % halves] += jnp.where(in_hole, 0.0, rest)
        sums[(n_block - 1) % halves] += jnp.where(in_hole, rest, 0.0)
    total = jnp.zeros((1, LANES), jnp.float32)
    for half in range(halves):
        energy = jnp.sum(sums[half], axis=1, keepdims=True)
        row = lax.broadcasted_iota(jnp.int32, (GROUP, LANES), 0) + half * GROUP
        lane = lax.broadcasted_iota(jnp.int32, (GROUP, LANES), 1)
        total += jnp.sum(jnp.where(lane % rows == row, energy, 0.0), axis=0, keepdims=True)
    message = total * weight_ref[...] + label_ref[...]
    message_ref[...] = jnp.broadcast_to(message, message_ref.shape)


def write_chi(high_ref, low_ref, times_ref, chi_ref, done):
    n_source = times_ref.shape[0]
    n_freq, rows, width = chi_ref.shape
    head, hole = own_place()
    turn = head * SHIFT
    quarter = lax.broadcasted_iota(jnp.int32, (GROUP, LANES), 1) // SHIFT
    wide = lax.broadcasted_iota(jnp.int32, (n_freq * GROUP, LANES), 1)
    n_block = NTAU // n_source * (rows // GROUP)

    def stored(i, tile):
        return times_ref[ORDER.index(i), pl.ds(tile * GROUP, GROUP), :]

    def last_rest(i):
        rest = stored(i, n_block * FULL)
        for m in range(FULL):
            moved = roll(stored(i, n_block * FULL + m), (1 + m) * SHIFT)
            rest = jnp.where(quarter == lax.rem(hole + 1 + m, QUARTERS), moved, rest)
        return rest

    def column_tile(half, m):
        parts = []
        for t in range(NTAU):
            i, tt = divmod(t, NTAU // n_source)
            q = tt * (rows // GROUP) + half
            if m < FULL:
                parts.append(stored(i, q * FULL + m))
            elif q < n_block - 1:
                parts.append(stored(i, n_block * FULL + q))
            else:
                parts.append(last_rest(i))
        return jnp.concatenate(parts, axis=0)

    for half in range(rows // GROUP):
        block = pl.ds(half * GROUP, GROUP)
        values = jnp.concatenate([column_tile(half, m) for m in range(FULL + 1)], axis=1)
        chi = transformed(high_ref, low_ref, values)
        turned = [pltpu.roll(chi[:, m * LANES : (m + 1) * LANES], turn, 1) for m in range(FULL + 1)]
        for m in range(FULL + 1):
            count = min(LANES, width - m * LANES)
            natural = jnp.where(wide < turn, turned[m - 1], turned[m])[:, :count]
            natural = natural.astype(jnp.bfloat16).reshape(n_freq, GROUP, count)
            chi_ref[:, block, pl.ds(m * LANES, count)] = natural
        done(half, block)


def forces_kernel(
    rows, n_col, message_ref, high_ref, low_ref, times_ref,
    forces_out_ref, chi_out_ref, forces_ref, chi_ref, sems,
):
    stores = []

    def send(half, block):
        store = pltpu.make_async_copy(chi_ref.at[:, block], chi_out_ref.at[:, block], sems.at[half])
        store.start()
        stores.append(store)

    write_chi(high_ref, low_ref, times_ref, chi_ref, send)
    n_pair = message_ref.shape[0] // n_col
    sums = []
    for pair in range(n_pair):
        total = message_ref[pair * n_col]
        for i in range(1, n_col):
            total += message_ref[pair * n_col + i]
        sums.append(total)
    sums = jnp.concatenate(sums, axis=0)
    n_block = n_pair * CORES
    block = lax.broadcasted_iota(jnp.int32, (n_block, LANES), 0)
    quarter = lax.broadcasted_iota(jnp.int32, (n_block, LANES), 1) // rows
    own = quarter == block % QUARTERS
    turned = [sums if d == 0 else pltpu.roll(sums, d * rows, 1) for d in range(QUARTERS)]

    def along_lanes(part):
        placed = jnp.zeros((n_block, LANES), jnp.float32)
        for d in range(QUARTERS):
            placed = jnp.where(own & (quarter == (part + d) % QUARTERS), turned[d], placed)
        tiles = [
            jnp.sum(jnp.where(block // QUARTERS == tile, placed, 0.0), axis=0, keepdims=True)
            for tile in range(n_block // QUARTERS)
        ]
        return jnp.concatenate(tiles, axis=1)

    owners = along_lanes(3).astype(jnp.int32)
    width = n_block * rows
    part = lax.broadcasted_iota(jnp.int32, (8, width), 0)
    weights = jnp.zeros((8, width), jnp.float32)
    for p in range(3):
        weights = jnp.where(part == p, along_lanes(p), weights)
    upper, lower = owners // LANES, owners % LANES
    n_upper = pl.cdiv(NATOM, LANES)
    lanes = lax.broadcasted_iota(jnp.int32, (LANES, width), 0)
    onehot = jnp.where(lanes == lower, 1.0, 0.0).astype(jnp.bfloat16)
    pieces = []
    rest = weights
    for _ in range(3):
        piece = rest.astype(jnp.bfloat16).astype(jnp.float32)
        rest = rest - piece
        pieces += [jnp.where(upper == u, piece, 0.0) for u in range(n_upper)]
    pieces = jnp.concatenate(pieces, axis=0).astype(jnp.bfloat16)
    products = lax.dot_general(
        pieces, onehot, (((1,), (1,)), ((), ())), preferred_element_type=jnp.float32
    )
    count = 8 * n_upper
    forces = products[:count] + products[count : 2 * count] + products[2 * count :]
    for u in range(n_upper):
        count = min(LANES, NATOM - u * LANES)
        forces_ref[:, u * LANES : u * LANES + count] = forces[u * 8 : u * 8 + 3, :count]
    store = pltpu.make_async_copy(forces_ref, forces_out_ref, sems.at[rows // GROUP])
    store.start()
    for store in [*stores, store]:
        store.wait()


def on_device(sizes, green_occ, green_virt, adjoint_w, grad_basis, owner_map, block_offset):
    n_pair, n_near, n_tm = sizes
    n_col = n_near * FAR
    n_time, rows, columns = green_occ.shape
    width = columns // n_tm
    high, low = (jnp.asarray(part) for part in transform_matrix())
    n_block = n_time * rows // GROUP
    tiles = n_block * FULL + FULL
    assert width == FULL * LANES + (QUARTERS - 1) * SHIFT and n_block == FULL + 1

    packed = (n_tm, tiles * GROUP, LANES)
    product = pl.pallas_call(
        product_kernel,
        in_specs=[pl.BlockSpec(memory_space=pl.ANY)] * 2,
        out_specs=pl.BlockSpec(memory_space=pl.ANY),
        out_shape=jax.ShapeDtypeStruct(packed, jnp.bfloat16),
        scratch_shapes=[
            pltpu.VMEM(green_occ.shape, jnp.bfloat16),
            pltpu.VMEM(green_virt.shape, jnp.bfloat16),
            pltpu.VMEM(packed, jnp.bfloat16),
            pltpu.SemaphoreType.DMA((n_block, 2)),
            pltpu.SemaphoreType.DMA((n_block,)),
        ],
        compiler_params=pltpu.CompilerParams(vmem_limit_bytes=60 << 20),
        name="product",
    )(green_occ, green_virt)
    times = lax.all_to_all(
        product, "tm", split_axis=0, concat_axis=0, tiled=True, axis_index_groups=[ORDER]
    )

    def kernel(body, name, shape, dtype, limit, *operands):
        elements = NTAU * rows * width
        return pl.pallas_call(
            body,
            out_shape=jax.ShapeDtypeStruct(shape, dtype),
            cost_estimate=pl.CostEstimate(
                flops=4 * NTAU * GROUP * elements, bytes_accessed=4 * elements, transcendentals=0
            ),
            compiler_params=pltpu.CompilerParams(vmem_limit_bytes=limit << 20),
            name=name,
        )(*operands)

    scale = 1.0 / math.sqrt(NTAU * NG)
    owners = lax.dynamic_slice_in_dim(owner_map, block_offset[0], rows, 0)
    weight = jnp.concatenate([grad_basis.reshape(3 * rows) * scale, jnp.zeros((rows,), jnp.float32)])
    label = jnp.concatenate(
        [jnp.zeros((3 * rows,), jnp.float32), owners.astype(jnp.float32) * (1.0 / (n_col * n_tm))]
    )
    adjoint = kernel(adjoint_kernel, "adjoint", packed, jnp.float32, 16, high, low, adjoint_w)
    message = pl.pallas_call(
        functools.partial(energy_kernel, rows),
        out_shape=jax.ShapeDtypeStruct((CORES * n_near * n_tm, LANES), jnp.float32),
        compiler_params=pltpu.CompilerParams(vmem_limit_bytes=16 << 20),
        name="energy",
    )(times, adjoint, weight[None, :], label[None, :])

    message = lax.all_to_all(message, ("core", "near", "tm"), split_axis=0, concat_axis=0, tiled=True)
    message = jnp.sum(message.reshape(CORES, n_near * n_tm, LANES), axis=1)
    message = jnp.broadcast_to(message[None], (n_pair * FAR, CORES, LANES))
    message = lax.all_to_all(message, ("pair", "far"), split_axis=0, concat_axis=0, tiled=True)
    shape = (NTAU, rows, width)
    forces, chi_freq = pl.pallas_call(
        functools.partial(forces_kernel, rows, FAR),
        out_specs=[pl.BlockSpec(memory_space=pl.ANY)] * 2,
        out_shape=(
            jax.ShapeDtypeStruct((3, NATOM), jnp.float32),
            jax.ShapeDtypeStruct(shape, jnp.bfloat16),
        ),
        scratch_shapes=[
            pltpu.VMEM((3, NATOM), jnp.float32),
            pltpu.VMEM(shape, jnp.bfloat16),
            pltpu.SemaphoreType.DMA((rows // GROUP + 1,)),
        ],
        compiler_params=pltpu.CompilerParams(vmem_limit_bytes=16 << 20),
        name="forces",
    )(message, high, low, times)
    return (chi_freq, forces)


def solution(mesh):
    n_row, n_col, n_tm = (mesh.shape[name] for name in ("row", "col", "tm"))
    n_pair = n_row // CORES
    n_near = n_col // FAR
    axes = ("pair", "core", "near", "far", "tm")
    fine = Mesh(mesh.devices.reshape(n_pair, CORES, n_near, FAR, n_tm), axes)
    row, col = ("pair", "core"), ("near", "far")
    in_specs = (
        P("tm", row, col),
        P("tm", row, col),
        P(None, row, col + ("tm",)),
        P(None, row),
        P(),
        P(row),
    )
    out_specs = (P(None, row, col + ("tm",)), P())
    return jax.shard_map(
        functools.partial(on_device, (n_pair, n_near, n_tm)),
        mesh=fine,
        in_specs=in_specs,
        out_specs=out_specs,
        check_vma=False,
    )
```

```python
import functools
import math

import jax
import jax.numpy as jnp
import ml_dtypes
import numpy as np
from jax import lax
from jax.experimental import pallas as pl
from jax.experimental.pallas import tpu as pltpu
from jax.sharding import Mesh, PartitionSpec as P

NG = 30720
NTAU = 16
NATOM = 1000
GROUP = 16
LANES = 128
SHIFT = 32
QUARTERS = LANES // SHIFT
FULL = 3
CORES = 2
FAR = 2


def transform_matrix():
    steps = np.arange(NTAU, dtype=np.float64)
    table = np.cos(0.1 * 0.15 * 1.35 ** (steps[:, None] + steps[None, :])) / 4.0
    high = table.astype(ml_dtypes.bfloat16)
    low = (table - high.astype(np.float64)).astype(ml_dtypes.bfloat16)
    eye = np.eye(GROUP)
    return [np.kron(part.astype(np.float64), eye).astype(ml_dtypes.bfloat16) for part in (high, low)]


def roll(values, shift):
    return pltpu.roll(values.astype(jnp.float32), shift, 1).astype(values.dtype)


def product_kernel(occ_ref, virt_ref, out_ref, occ, virt, out, in_sems, out_sems):
    n_dest = out_ref.shape[0]
    n_time, rows, _ = occ.shape
    blocks = [(t, pl.ds(start, GROUP)) for t in range(n_time) for start in range(0, rows, GROUP)]
    loads, stores = [], []
    for q, (t, block) in enumerate(blocks):
        pair = [
            pltpu.make_async_copy(src.at[t, block], dst.at[t, block], in_sems.at[q, s])
            for s, (src, dst) in enumerate(((occ_ref, occ), (virt_ref, virt)))
        ]
        for load in pair:
            load.start()
        loads.append(pair)

    def send(part, first, count):
        rows = pl.ds(first * GROUP, count * GROUP)
        store = pltpu.make_async_copy(out.at[:, rows], out_ref.at[:, rows], out_sems.at[part])
        store.start()
        stores.append(store)

    quarter = lax.broadcasted_iota(jnp.int32, (GROUP, LANES), 1) // SHIFT
    rests = {}
    for q, (t, block) in enumerate(blocks):
        for load in loads[q]:
            load.wait()

        def tile(k):
            columns = pl.ds(k * LANES, LANES)
            return occ[t, block, columns] * virt[t, block, columns]

        for j in range(n_dest):
            start = j * (FULL * QUARTERS + QUARTERS - 1)
            head = -start % QUARTERS
            hole = QUARTERS - 1 - head
            first = (start + head) // QUARTERS
            for m in range(FULL):
                out[j, pl.ds((q * FULL + m) * GROUP, GROUP), :] = tile(first + m)
            if head == 0:
                rest = tile(first + FULL)
            elif hole == 0:
                rest = tile(first - 1)
            else:
                rest = jnp.where(quarter > hole, tile(first - 1), tile(first + FULL))
            rests[j, q] = rest
        if q < len(blocks) - 1:
            send(q, q * FULL, FULL)
            continue
        for j in range(n_dest):
            hole = QUARTERS - 1 - -j * (FULL * QUARTERS + QUARTERS - 1) % QUARTERS
            for m in range(FULL):
                moved = roll(rests[j, q], LANES - (1 + m) * SHIFT)
                filled = jnp.where(quarter == hole, moved, rests[j, m])
                out[j, pl.ds(((q + 1) * FULL + m) * GROUP, GROUP), :] = filled
        send(q, q * FULL, 2 * FULL)
    for store in stores:
        store.wait()


def own_place():
    head = lax.rem(lax.axis_index("tm"), QUARTERS)
    return head, QUARTERS - 1 - head


def transformed(high_ref, low_ref, values):
    total = jnp.dot(high_ref[...], values, preferred_element_type=jnp.float32)
    return total + jnp.dot(low_ref[...], values, preferred_element_type=jnp.float32)


def adjoint_kernel(high_ref, low_ref, adjoint_ref, out_ref):
    n_freq, rows, width = adjoint_ref.shape
    n_source = out_ref.shape[0]
    per_source, halves = n_freq // n_source, rows // GROUP
    n_block = per_source * halves
    head, hole = own_place()
    split = LANES - head * SHIFT
    quarter = lax.broadcasted_iota(jnp.int32, (GROUP, LANES), 1) // SHIFT
    wide = lax.broadcasted_iota(jnp.int32, (n_freq * GROUP, LANES), 1)
    rests = {}
    for half in range(halves):
        block = pl.ds(half * GROUP, GROUP)
        values = adjoint_ref[:, block, :].reshape(n_freq * GROUP, width)
        total = transformed(high_ref, low_ref, values)
        pad = jnp.zeros((n_freq * GROUP, (FULL + 1) * LANES - width), jnp.float32)
        total = jnp.concatenate([total, pad], axis=1)
        turned = [
            pltpu.roll(total[:, m * LANES : (m + 1) * LANES], lax.rem(split, LANES), 1)
            for m in range(FULL + 1)
        ]
        packed = [jnp.where(wide < split, turned[m], turned[m + 1]) for m in range(FULL)]
        rest = jnp.where(wide < split, turned[FULL], turned[0])
        for t in range(n_freq):
            i, tt = divmod(t, per_source)
            q = tt * halves + half
            lines = slice(t * GROUP, (t + 1) * GROUP)
            for m in range(FULL):
                out_ref[i, pl.ds((q * FULL + m) * GROUP, GROUP), :] = packed[m][lines]
            rests[i, q] = rest[lines]
    for i in range(n_source):
        for m in range(FULL):
            moved = pltpu.roll(rests[i, n_block - 1], LANES - (1 + m) * SHIFT, 1)
            filled = jnp.where(quarter == hole, moved, rests[i, m])
            out_ref[i, pl.ds((n_block * FULL + m) * GROUP, GROUP), :] = filled


def energy_kernel(rows, times_ref, adjoint_ref, weight_ref, label_ref, message_ref):
    n_source, lines, _ = times_ref.shape
    n_block = lines // GROUP // FULL - 1
    halves = rows // GROUP
    _, hole = own_place()
    in_hole = lax.broadcasted_iota(jnp.int32, (GROUP, LANES), 1) // SHIFT == hole
    sums = [jnp.zeros((GROUP, LANES), jnp.float32) for _ in range(halves)]

    def terms(tile):
        lines = pl.ds(tile * GROUP, GROUP)
        total = jnp.zeros((GROUP, LANES), jnp.float32)
        for i in range(n_source):
            total += times_ref[i, lines, :].astype(jnp.float32) * adjoint_ref[i, lines, :]
        return total

    for q in range(n_block):
        for m in range(FULL):
            sums[q % halves] += terms(q * FULL + m)
    for m in range(FULL):
        rest = terms(n_block * FULL + m)
        sums[m % halves] += jnp.where(in_hole, 0.0, rest)
        sums[(n_block - 1) % halves] += jnp.where(in_hole, rest, 0.0)
    total = jnp.zeros((1, LANES), jnp.float32)
    for half in range(halves):
        energy = jnp.sum(sums[half], axis=1, keepdims=True)
        row = lax.broadcasted_iota(jnp.int32, (GROUP, LANES), 0) + half * GROUP
        lane = lax.broadcasted_iota(jnp.int32, (GROUP, LANES), 1)
        total += jnp.sum(jnp.where(lane % rows == row, energy, 0.0), axis=0, keepdims=True)
    message = total * weight_ref[...] + label_ref[...]
    message_ref[...] = jnp.broadcast_to(message, message_ref.shape)


def write_chi(high_ref, low_ref, times_ref, chi_ref, done):
    n_source = times_ref.shape[0]
    n_freq, rows, width = chi_ref.shape
    head, hole = own_place()
    turn = head * SHIFT
    quarter = lax.broadcasted_iota(jnp.int32, (GROUP, LANES), 1) // SHIFT
    wide = lax.broadcasted_iota(jnp.int32, (n_freq * GROUP, LANES), 1)
    n_block = NTAU // n_source * (rows // GROUP)

    def stored(i, tile):
        return times_ref[i, pl.ds(tile * GROUP, GROUP), :]

    def last_rest(i):
        rest = stored(i, n_block * FULL)
        for m in range(FULL):
            moved = roll(stored(i, n_block * FULL + m), (1 + m) * SHIFT)
            rest = jnp.where(quarter == lax.rem(hole + 1 + m, QUARTERS), moved, rest)
        return rest

    def column_tile(half, m):
        parts = []
        for t in range(NTAU):
            i, tt = divmod(t, NTAU // n_source)
            q = tt * (rows // GROUP) + half
            if m < FULL:
                parts.append(stored(i, q * FULL + m))
            elif q < n_block - 1:
                parts.append(stored(i, n_block * FULL + q))
            else:
                parts.append(last_rest(i))
        return jnp.concatenate(parts, axis=0)

    for half in range(rows // GROUP):
        block = pl.ds(half * GROUP, GROUP)
        values = jnp.concatenate([column_tile(half, m) for m in range(FULL + 1)], axis=1)
        chi = transformed(high_ref, low_ref, values)
        turned = [pltpu.roll(chi[:, m * LANES : (m + 1) * LANES], turn, 1) for m in range(FULL + 1)]
        for m in range(FULL + 1):
            count = min(LANES, width - m * LANES)
            natural = jnp.where(wide < turn, turned[m - 1], turned[m])[:, :count]
            natural = natural.astype(jnp.bfloat16).reshape(n_freq, GROUP, count)
            chi_ref[:, block, pl.ds(m * LANES, count)] = natural
        done(half, block)


def forces_kernel(
    rows, n_col, message_ref, high_ref, low_ref, times_ref,
    forces_out_ref, chi_out_ref, forces_ref, chi_ref, sems,
):
    stores = []

    def send(half, block):
        store = pltpu.make_async_copy(chi_ref.at[:, block], chi_out_ref.at[:, block], sems.at[half])
        store.start()
        stores.append(store)

    write_chi(high_ref, low_ref, times_ref, chi_ref, send)
    sums = []
    for block in range(message_ref.shape[0] // n_col * CORES):
        pair, core = divmod(block, CORES)
        devices = pl.ds(pair * n_col, n_col)
        sums.append(jnp.sum(message_ref[devices, core, :], axis=0, keepdims=True))
    parts = [
        jnp.concatenate([total[:, p * rows : (p + 1) * rows] for total in sums], axis=1)
        for p in range(4)
    ]
    owners = parts[3].astype(jnp.int32)
    weights = jnp.concatenate(parts[:3] + [jnp.zeros_like(parts[0])] * 5, axis=0)
    upper, lower = owners // LANES, owners % LANES
    n_upper = pl.cdiv(NATOM, LANES)
    rest = jnp.concatenate([jnp.where(upper == u, weights, 0.0) for u in range(n_upper)], axis=0)
    lanes = lax.broadcasted_iota(jnp.int32, (LANES, owners.shape[1]), 0)
    onehot = jnp.where(lanes == lower, 1.0, 0.0).astype(jnp.bfloat16)
    forces = jnp.zeros((8 * n_upper, LANES), jnp.float32)
    for _ in range(3):
        part = rest.astype(jnp.bfloat16)
        rest = rest - part.astype(jnp.float32)
        forces += lax.dot_general(
            part, onehot, (((1,), (1,)), ((), ())), preferred_element_type=jnp.float32
        )
    for u in range(n_upper):
        count = min(LANES, NATOM - u * LANES)
        forces_ref[:, u * LANES : u * LANES + count] = forces[u * 8 : u * 8 + 3, :count]
    store = pltpu.make_async_copy(forces_ref, forces_out_ref, sems.at[rows // GROUP])
    store.start()
    for store in [*stores, store]:
        store.wait()


def on_device(sizes, green_occ, green_virt, adjoint_w, grad_basis, owner_map, block_offset):
    n_pair, n_near, n_tm = sizes
    n_col = n_near * FAR
    n_time, rows, columns = green_occ.shape
    width = columns // n_tm
    high, low = (jnp.asarray(part) for part in transform_matrix())
    n_block = n_time * rows // GROUP
    tiles = n_block * FULL + FULL
    assert width == FULL * LANES + (QUARTERS - 1) * SHIFT and n_block == FULL + 1

    packed = (n_tm, tiles * GROUP, LANES)
    product = pl.pallas_call(
        product_kernel,
        in_specs=[pl.BlockSpec(memory_space=pl.ANY)] * 2,
        out_specs=pl.BlockSpec(memory_space=pl.ANY),
        out_shape=jax.ShapeDtypeStruct(packed, jnp.bfloat16),
        scratch_shapes=[
            pltpu.VMEM(green_occ.shape, jnp.bfloat16),
            pltpu.VMEM(green_virt.shape, jnp.bfloat16),
            pltpu.VMEM(packed, jnp.bfloat16),
            pltpu.SemaphoreType.DMA((n_block, 2)),
            pltpu.SemaphoreType.DMA((n_block,)),
        ],
        compiler_params=pltpu.CompilerParams(vmem_limit_bytes=60 << 20),
        name="product",
    )(green_occ, green_virt)
    times = lax.all_to_all(product, "tm", split_axis=0, concat_axis=0, tiled=True)

    def kernel(body, name, shape, dtype, limit, *operands):
        elements = NTAU * rows * width
        return pl.pallas_call(
            body,
            out_shape=jax.ShapeDtypeStruct(shape, dtype),
            cost_estimate=pl.CostEstimate(
                flops=4 * NTAU * GROUP * elements, bytes_accessed=4 * elements, transcendentals=0
            ),
            compiler_params=pltpu.CompilerParams(vmem_limit_bytes=limit << 20),
            name=name,
        )(*operands)

    scale = 1.0 / math.sqrt(NTAU * NG)
    owners = lax.dynamic_slice_in_dim(owner_map, block_offset[0], rows, 0)
    weight = jnp.concatenate([grad_basis.reshape(3 * rows) * scale, jnp.zeros((rows,), jnp.float32)])
    label = jnp.concatenate(
        [jnp.zeros((3 * rows,), jnp.float32), owners.astype(jnp.float32) * (1.0 / (n_col * n_tm))]
    )
    adjoint = kernel(adjoint_kernel, "adjoint", packed, jnp.float32, 16, high, low, adjoint_w)
    message = pl.pallas_call(
        functools.partial(energy_kernel, rows),
        out_shape=jax.ShapeDtypeStruct((CORES * n_near, LANES), jnp.float32),
        compiler_params=pltpu.CompilerParams(vmem_limit_bytes=16 << 20),
        name="energy",
    )(times, adjoint, weight[None, :], label[None, :])

    message = lax.all_to_all(message, ("core", "near"), split_axis=0, concat_axis=0, tiled=True)
    message = jnp.sum(message.reshape(CORES, n_near, LANES), axis=1)
    message = jnp.broadcast_to(message[None], (n_pair * FAR * n_tm, CORES, LANES))
    message = lax.all_to_all(message, ("pair", "far", "tm"), split_axis=0, concat_axis=0, tiled=True)
    shape = (NTAU, rows, width)
    forces, chi_freq = pl.pallas_call(
        functools.partial(forces_kernel, rows, FAR * n_tm),
        out_specs=[pl.BlockSpec(memory_space=pl.ANY)] * 2,
        out_shape=(
            jax.ShapeDtypeStruct((3, NATOM), jnp.float32),
            jax.ShapeDtypeStruct(shape, jnp.bfloat16),
        ),
        scratch_shapes=[
            pltpu.VMEM((3, NATOM), jnp.float32),
            pltpu.VMEM(shape, jnp.bfloat16),
            pltpu.SemaphoreType.DMA((rows // GROUP + 1,)),
        ],
        compiler_params=pltpu.CompilerParams(vmem_limit_bytes=16 << 20),
        name="forces",
    )(message, high, low, times)
    return (chi_freq, forces)


def solution(mesh):
    n_row, n_col, n_tm = (mesh.shape[name] for name in ("row", "col", "tm"))
    n_pair = n_row // CORES
    n_near = n_col // FAR
    axes = ("pair", "core", "near", "far", "tm")
    fine = Mesh(mesh.devices.reshape(n_pair, CORES, n_near, FAR, n_tm), axes)
    row, col = ("pair", "core"), ("near", "far")
    in_specs = (
        P("tm", row, col),
        P("tm", row, col),
        P(None, row, col + ("tm",)),
        P(None, row),
        P(),
        P(row),
    )
    out_specs = (P(None, row, col + ("tm",)), P())
    return jax.shard_map(
        functools.partial(on_device, (n_pair, n_near, n_tm)),
        mesh=fine,
        in_specs=in_specs,
        out_specs=out_specs,
        check_vma=False,
    )
```
